512 devices in a mesh: cell: 32 (over y, z_hi), sensor: 16 (over z_lo, x, core).
Axes of the slice: x: 4, y: 8, z: 8 (z_hi: 4, z_lo: 2; z = z_hi * 2 + z_lo), core: 2. Of those that a mesh axis runs over, the one named last changes fastest.
Arguments:
- kernel: bfloat16 [2, 65, 1024, 8192], P(None, None, 'sensor', 'cell'), may hold values from -3 to 3
- observed: float32 [64, 1024], P(None, 'sensor'), may hold values from -6 to 6
- start_model: float32 [64, 8192], P(None, 'cell'), may hold values from -6 to 6
- start_multiplier: float32 [4, 64, 8192], P(None, None, 'cell'), may hold values from -1.8 to 1.8
- neighbours: int32 [4, 8192], P(None, 'cell'), may hold values from 0 to 8191, as said below
- tile_of_cell: int32 [8192], P('cell'), may hold values from 0 to 63
- tile_weight: float32 [64], replicated, may hold values from 0.3 to 3
Outputs:
- estimate: float32 [64, 8192], P(None, 'cell')
- auxiliary: float32 [4, 64, 8192], P(None, None, 'cell')
- multiplier: float32 [4, 64, 8192], P(None, None, 'cell')
The draws below stay inside these ranges and needn't reach their ends.
Inputs may be any that keep to these rules, and one draw needn't show every extreme that they name: The cells form a grid of 64 rows of 128 cells, numbered row by row. neighbours[k, c] is c itself or the cell beside c: c + 1 for k = 0 and c - 1 for k = 1 within the same row, c - 128 for k = 2 and c + 128 for k = 3. Where neighbours[k, c] = c' differs from c, neighbours[k xor 1, c'] = c.
All inputs are finite; a program needn't handle non-finite values.
Results may differ from the reference program's by a relative error of at most 0.00092.
Values sent between devices are 32-bit elements; how exact they have to be, the bound alone decides.
A program may use at most 64 MiB of HBM per device.

```python
import math
import jax
import jax.numpy as jnp
from jax import lax

NT = 64
NF = 65
COLS = 128
TILES = 64
ITERS = 2
NC = 8192
NS = 1024


def draw_kernel(key, part):
    noise = jnp.clip(jax.random.normal(key, (2, NF, NS, NC), jnp.float32), -6.0, 6.0)
    cell_ramp = 0.5 + 1.5 * jnp.arange(NC).astype(jnp.float32) / NC
    sensor_ramp = 0.6 + 1.2 * jnp.arange(NS).astype(jnp.float32) / NS
    scaled = noise * cell_ramp[None, None, None, :] * sensor_ramp[None, None, :, None]
    return (scaled / NC ** 0.5).astype(jnp.bfloat16)


def draw_neighbours(key, part):
    row_count = NC // COLS
    first_key = jax.random.fold_in(key, 11)
    second_key = jax.random.fold_in(key, 13)
    cut_along = jax.random.randint(first_key, (row_count, COLS), 0, 100) < 15
    cut_across = jax.random.randint(second_key, (row_count, COLS), 0, 100) < 15
    row_index = lax.broadcasted_iota(jnp.int32, (row_count, COLS), 0)
    col_index = lax.broadcasted_iota(jnp.int32, (row_count, COLS), 1)
    cell_number = row_index * COLS + col_index
    east = jnp.where((col_index < COLS - 1) & jnp.logical_not(cut_along), cell_number + 1, cell_number)
    west = jnp.where((col_index > 0) & jnp.logical_not(jnp.roll(cut_along, 1, axis=1)), cell_number - 1, cell_number)
    north = jnp.where((row_index > 0) & jnp.logical_not(jnp.roll(cut_across, 1, axis=0)), cell_number - COLS, cell_number)
    south = jnp.where((row_index < row_count - 1) & jnp.logical_not(cut_across), cell_number + COLS, cell_number)
    return jnp.stack([east, west, north, south]).reshape(4, NC).astype(jnp.int32)


def plant(drawn, key, least, top_value):
    shape = drawn.shape
    spot = [jax.random.randint(jax.random.fold_in(key, axis), (), 0, shape[axis]) for axis in range(len(shape))]
    drawn = drawn.at[tuple(spot)].set(least)
    longest = shape.index(max(shape))
    spot[longest] = (spot[longest] + 1) % shape[longest]
    return drawn.at[tuple(spot)].set(top_value)


def steps_of(own_key, extent, pieces, low, high):
    level = 1.0
    for axis_at, shards_of in pieces:
        heights = jax.random.uniform(jax.random.fold_in(jax.random.fold_in(own_key, 6), axis_at), (shards_of,), jnp.float32, low / len(pieces), high / len(pieces))
        level = level * jnp.repeat(jnp.exp(heights), extent[axis_at] // shards_of).reshape((-1,) + (1,) * (len(extent) - 1 - axis_at))
    return level


def gaussian(rng, dims, width, limit, cuts=(), held_as=jnp.bfloat16):
    drawn = jax.random.normal(rng, dims, jnp.float32) * width
    if len(cuts) > 0:
        drawn = steps_of(rng, dims, cuts, -0.22, 0.18) * drawn
    return jnp.clip(drawn, min=-limit, max=limit).astype(held_as)


def setup_inputs(seed: int = 0) -> dict:
    arg_keys = jax.random.split(jax.random.key(seed), 8)
    kernel = draw_kernel(jax.random.fold_in(arg_keys[7], 71), 0)
    observed = gaussian(arg_keys[1], (NT, NS), 1.0, 6.0, ((1, 16),), jnp.float32)
    start_model = gaussian(arg_keys[2], (NT, NC), 1.0, 6.0, ((1, 32),), jnp.float32)
    start_multiplier = gaussian(arg_keys[3], (4, NT, NC), 0.3, 1.8, ((2, 32),), jnp.float32)
    neighbours = draw_neighbours(jax.random.fold_in(arg_keys[7], 71), 0)
    tile_of_cell = plant(jax.random.randint(arg_keys[5], (NC,), 0, TILES), jax.random.fold_in(arg_keys[5], 1), 0, TILES - 1).astype(jnp.int32)
    tile_weight = jnp.clip(jnp.exp(jax.random.uniform(arg_keys[6], (TILES,), jnp.float32, math.log(0.3), math.log(3.0))), 0.3, 3.0)
    return {"kernel": kernel, "observed": observed, "start_model": start_model, "start_multiplier": start_multiplier, "neighbours": neighbours, "tile_of_cell": tile_of_cell, "tile_weight": tile_weight}


SHRINK_SCALE = 0.4
TINY = 1e-6


def exact_dot(left, right):
    return jnp.dot(left, right, precision=lax.Precision.HIGHEST, preferred_element_type=jnp.float32)


def tables(times_count, freq_count):
    padded = 2 * times_count
    freq_index = lax.broadcasted_iota(jnp.int32, (freq_count, times_count), 0)
    time_index = lax.broadcasted_iota(jnp.int32, (freq_count, times_count), 1)
    phase = ((freq_index * time_index) % padded).astype(jnp.float32) * (2.0 * jnp.pi / padded)
    cosine = jnp.cos(phase)
    sine_table = jnp.sin(phase)
    weight = jnp.where((freq_index == 0) | (freq_index == freq_count - 1), 1.0, 2.0).astype(jnp.float32) / padded
    return cosine, sine_table, cosine * weight, sine_table * weight


def forward(kernel, series, tabs):
    cosine, sine_table, cos_weighted, sin_weighted = tabs
    real_part = exact_dot(cosine, series).astype(jnp.bfloat16)
    imag_part = (-exact_dot(sine_table, series)).astype(jnp.bfloat16)

    def per_frequency(index):
        slab = lax.dynamic_index_in_dim(kernel, index, 1, keepdims=False).astype(jnp.float32)
        real_in = lax.dynamic_index_in_dim(real_part, index, 0, keepdims=False).astype(jnp.float32)
        imag_in = lax.dynamic_index_in_dim(imag_part, index, 0, keepdims=False).astype(jnp.float32)
        out_real = exact_dot(slab[0], real_in) - exact_dot(slab[1], imag_in)
        out_imag = exact_dot(slab[0], imag_in) + exact_dot(slab[1], real_in)
        return out_real, out_imag

    out_real, out_imag = lax.map(per_frequency, jnp.arange(NF).astype(jnp.int32))
    return exact_dot(cos_weighted.T, out_real) - exact_dot(sin_weighted.T, out_imag)


def adjoint(kernel, misfit, tabs):
    cosine, sine_table, cos_weighted, sin_weighted = tabs
    back_real = exact_dot(cos_weighted, misfit).astype(jnp.bfloat16)
    back_imag = (-exact_dot(sin_weighted, misfit)).astype(jnp.bfloat16)

    def per_frequency(index):
        slab = lax.dynamic_index_in_dim(kernel, index, 1, keepdims=False).astype(jnp.float32)
        real_in = lax.dynamic_index_in_dim(back_real, index, 0, keepdims=False).astype(jnp.float32)
        imag_in = lax.dynamic_index_in_dim(back_imag, index, 0, keepdims=False).astype(jnp.float32)
        spec_real = exact_dot(real_in, slab[0]) + exact_dot(imag_in, slab[1])
        spec_imag = exact_dot(imag_in, slab[0]) - exact_dot(real_in, slab[1])
        return spec_real, spec_imag

    spec_real, spec_imag = lax.map(per_frequency, jnp.arange(NF).astype(jnp.int32))
    return exact_dot(cosine.T, spec_real) - exact_dot(sine_table.T, spec_imag)


def differences(series, neighbours):
    return jnp.stack([series[:, neighbours[direction]] for direction in range(4)]) - series[None]


def transposed_differences(values, neighbours, linked):
    masked = values * linked[:, None, :]
    outgoing = jnp.sum(masked, axis=0)
    flat = jnp.transpose(masked, (0, 2, 1)).reshape(4 * NC, NT)
    incoming = jax.ops.segment_sum(flat, neighbours.reshape(-1), num_segments=NC)
    return incoming.T - outgoing


def reference(kernel, observed, start_model, start_multiplier, neighbours, tile_of_cell, tile_weight):
    tabs = tables(NT, NF)
    cell_index = jnp.arange(NC).astype(jnp.int32)
    linked = (neighbours != cell_index[None, :]).astype(jnp.float32)
    threshold = SHRINK_SCALE * tile_weight[tile_of_cell]
    estimate = start_model
    multiplier = start_multiplier
    model_jumps = differences(estimate, neighbours)
    auxiliary = model_jumps
    predicted = forward(kernel, estimate, tabs)
    for iteration in range(ITERS):
        penalty = model_jumps - auxiliary + multiplier
        gradient = adjoint(kernel, predicted - observed, tabs) + transposed_differences(penalty, neighbours, linked)
        response = forward(kernel, gradient, tabs)
        grad_jumps = differences(gradient, neighbours)
        grad_square = jnp.sum(gradient * gradient)
        response_square = jnp.sum(response * response)
        jump_square = jnp.sum(grad_jumps * grad_jumps)
        step_size = grad_square / (response_square + jump_square + TINY)
        estimate = estimate - step_size * gradient
        predicted = predicted - step_size * response
        model_jumps = model_jumps - step_size * grad_jumps
        shifted = model_jumps + multiplier
        auxiliary = jnp.sign(shifted) * jnp.maximum(jnp.abs(shifted) - threshold, 0.0)
        multiplier = shifted - auxiliary
    return estimate, auxiliary, multiplier
```

```python
import functools

import jax
import jax.numpy as jnp
import numpy as np
from jax import lax
from jax.experimental import pallas as pl
from jax.experimental.pallas import tpu as pltpu
from jax.sharding import Mesh
from jax.sharding import PartitionSpec as P

NT = 64
NF = 65
ROW = 128
NY = 8
NZ = 4
NSEN = 16
ROWS = 144
SHRINK_SCALE = 0.4
TINY = 1e-06
F32 = jnp.float32
BF16 = jnp.bfloat16
MESH = pl.DeviceIdType.MESH
Y_ORDER = (4, 3, 5, 2, 6, 1, 7)
Z_ORDER = (2, 1, 3)


def high_low(table):
    high = table.astype(BF16)
    low = (table - high.astype(np.float32)).astype(BF16)
    return high, low


def tables():
    freq = np.arange(NF)[:, None]
    time = np.arange(NT)[None, :]
    phase = 2.0 * np.pi * (freq * time % (2 * NT)) / (2 * NT)
    cosine, sine = np.cos(phase), np.sin(phase)
    weight = np.where((freq == 0) | (freq == NF - 1), 1.0, 2.0) / (2 * NT)
    wcos, wsin = cosine * weight, sine * weight

    def interleaved(even, odd):
        out = np.zeros((ROWS, NT), np.float32)
        out[0 : 2 * NF : 2] = even
        out[1 : 2 * NF : 2] = odd
        return out

    analysis = interleaved(cosine, -sine)
    back = np.concatenate([interleaved(wcos, -wsin), interleaved(-wsin, -wcos)], axis=0)
    synthesis = np.concatenate([interleaved(wcos, -wsin).T, interleaved(wsin, wcos).T], axis=0)
    ah, al = high_low(analysis)
    bh, bl = high_low(back)
    sh, sl = high_low(synthesis)
    ch, cl = high_low(analysis.T)
    return (
        np.concatenate([ah, al, ah, al], axis=1),
        np.concatenate([bh, bl, bh, bl], axis=1),
        np.stack([sh, sl]),
        np.stack([ch, cl]),
    )


def split(value):
    high = value.astype(BF16)
    return high, (value - high.astype(F32)).astype(BF16)


def dot(left, right, dims=((1,), (0,))):
    return lax.dot_general(left, right, (dims, ((), ())), preferred_element_type=F32)


def dot3(table_ref, value):
    high, low = split(value)
    th = table_ref[0]
    return dot(th, high) + dot(th, low) + dot(table_ref[1], high)


def stacked(value):
    high, low = split(value)
    return jnp.concatenate([high, high, low, low], axis=0)


def body(
    k_hbm, obs_ref, x0_ref, m0_ref, nb_ref, tile_ref, w_ref, tf_ref, ta_ref, ti_ref, ts_ref,
    est_ref, aux_ref, mul_ref,
    kv, m_s, ab_s, l_s, q_s,
    send1, ya, zb, za, yb, mid_a, mid_b,
    sc_send, sc_mid, sy, sz, rs_send, rs_buf,
    gp, rs_in, g_s, b_s, dt_s, thr_s, h_n, h_s, gh_n, gh_s,
    jump_s, gj_s, mult_s,
    k_sem, h_ssem, h_rsem, ar_ssem, ar_rsem, sc_ssem, sc_rsem, rs_ssem, rs_rsem, gr_ssem, gr_rsem,
    gh_ssem, gh_rsem,
):
    my = lax.axis_index("y")
    mz = lax.axis_index("zh")
    ms = lax.axis_index("sensor")
    cell = my * NZ + mz
    nxt = (cell + 1) % (NY * NZ)
    prv = (cell + NY * NZ - 1) % (NY * NZ)
    nxt_id = {"y": nxt // NZ, "zh": nxt % NZ}
    prv_id = {"y": prv // NZ, "zh": prv % NZ}
    y_ids = [{"y": (my + j) % NY} for j in Y_ORDER]
    z_ids = [{"zh": (mz + j) % NZ} for j in Z_ORDER]
    s_nums = [(ms + j) % NSEN for j in (7, 9, 6, 10, 5, 11, 4, 12, 3, 13, 8, 2, 14, 1, 15)]

    barrier = pltpu.get_barrier_semaphore()
    everyone = y_ids + z_ids + [{"sensor": p} for p in s_nums] + [nxt_id, prv_id]
    for who in everyone:
        pl.semaphore_signal(barrier, inc=1, device_id=who, device_id_type=MESH)

    bounds = (0, 16, 32, 48, 65)

    def k_copy(plane, q):
        lo, hi = bounds[q], bounds[q + 1]
        return pltpu.make_async_copy(
            k_hbm.at[plane, pl.ds(lo, hi - lo)],
            kv.at[pl.ds(lo, hi - lo), pl.ds(64 * plane, 64)],
            k_sem.at[plane, q],
        )

    for q in range(4):
        for plane in range(2):
            k_copy(plane, q).start()

    def send(src, dst, who, ssem, rsem):
        pltpu.make_async_remote_copy(
            src_ref=src, dst_ref=dst, send_sem=ssem, recv_sem=rsem, device_id=who,
            device_id_type=MESH,
        ).start()

    def wait_for(view, sem):
        pltpu.make_async_copy(view, view, sem).wait()

    lane = lax.broadcasted_iota(jnp.int32, (1, ROW), 1)
    left_half = lane < 64

    column = jnp.sum(
        jnp.where(
            lax.broadcasted_iota(jnp.int32, (64, 64), 0)
            == lax.broadcasted_iota(jnp.int32, (64, 64), 1),
            jnp.broadcast_to(w_ref[...], (64, 64)), 0.0,
        ),
        axis=1, keepdims=True,
    )
    labels = lax.broadcasted_iota(jnp.int32, (64, 2 * ROW), 0)
    threshold = SHRINK_SCALE * jnp.sum(
        jnp.where(labels == tile_ref[...], column, 0.0), axis=0, keepdims=True
    )
    thr_s[0] = jnp.broadcast_to(threshold[:, :ROW], (8, ROW))
    thr_s[1] = jnp.broadcast_to(threshold[:, ROW:], (8, ROW))
    own = cell * (2 * ROW) + lax.broadcasted_iota(jnp.int32, (1, 2 * ROW), 1)
    linked = [[None, None] for _ in range(4)]
    for k in range(4):
        both = jnp.where(nb_ref[pl.ds(k, 1), :] != own, 1.0, 0.0)
        linked[k][0] = both[:, :ROW] > 0.5
        linked[k][1] = both[:, ROW:] > 0.5

    group_row = lax.broadcasted_iota(jnp.int32, (8, ROW), 0) // 2

    def forward(field, first):
        m_s[...] = dot(tf_ref[...], stacked(field))

        def step(i, carry):
            moved = m_s[pl.ds(pl.multiple_of(8 * i, 8), 8), :].astype(BF16)
            weights = kv[pl.ds(4 * i, 4)].reshape(512, 256)
            out = dot(moved, weights, ((1,), (1,)))
            kept = out[:, 0:ROW]
            for j in range(1, 4):
                kept = jnp.where(group_row == j, out[:, j * ROW : (j + 1) * ROW], kept)
            ab_s[pl.ds(pl.multiple_of(8 * i, 8), 8), :] = kept
            return carry

        if first:
            for q in range(4):
                k_copy(0, q).wait()
                k_copy(1, q).wait()
                lax.fori_loop(4 * q, 4 * q + 4, step, 0, unroll=2)
        else:
            lax.fori_loop(0, 16, step, 0, unroll=2)
        tail = m_s[128:136, :].astype(BF16)
        ab_s[128:136, :] = dot(tail, kv[64], ((1,), (1,)))
        ab_s[136:144, :] = jnp.zeros((8, ROW), F32)
        out = dot3(ti_ref, ab_s[...])
        low = out[0:32] - pltpu.roll(out[64:96], 64, 1)
        high = pltpu.roll(out[32:64], 64, 1) - out[96:128]
        return jnp.where(left_half, low, high)

    def adjoint(packed, dst):
        turned = pltpu.roll(packed, 64, 1)
        doubled = jnp.concatenate(
            [jnp.where(left_half, packed, turned), jnp.where(left_half, turned, packed)], axis=0
        )
        out = dot(ta_ref[...], stacked(doubled))
        l_s[...] = jnp.where(left_half, out[:ROWS], out[ROWS:])

        def step(i, carry):
            rows = l_s[pl.ds(pl.multiple_of(8 * i, 8), 8), :]
            moved = jnp.concatenate(
                [jnp.where(group_row == j, rows, 0.0) for j in range(4)], axis=1
            ).astype(BF16)
            weights = kv[pl.ds(4 * i, 4)].reshape(512, 256)
            q_s[pl.ds(pl.multiple_of(8 * i, 8), 8), :] = dot(moved, weights)
            return carry

        lax.fori_loop(0, 16, step, 0, unroll=2)
        q_s[128:136, :] = dot(l_s[128:136, :].astype(BF16), kv[64])
        q_s[136:144, :] = jnp.zeros((8, 256), F32)
        out = dot3(ts_ref, q_s[...])
        dst[0:8] = out[:, :ROW].reshape(8, 8, ROW)
        dst[8:16] = out[:, ROW:].reshape(8, 8, ROW)

    def sum_start(n, packed):
        send1[n] = packed
        ya[n, my] = packed[0:16]
        zb[n, mz] = packed[16:32]
        for who in y_ids:
            send(send1.at[n, pl.ds(0, 16)], ya.at[n, my], who, ar_ssem.at[n, 0], ar_rsem.at[n, 0])
        for who in z_ids:
            send(send1.at[n, pl.ds(16, 16)], zb.at[n, mz], who, ar_ssem.at[n, 1], ar_rsem.at[n, 1])

    def sum_middle(n):
        wait_for(zb.at[n, pl.ds(0, NZ - 1)], ar_rsem.at[n, 1])
        part = jnp.sum(zb[n], axis=0)
        mid_b[n] = part
        yb[n, my] = part
        for who in y_ids:
            send(mid_b.at[n], yb.at[n, my], who, ar_ssem.at[n, 2], ar_rsem.at[n, 2])
        wait_for(ya.at[n, pl.ds(0, NY - 1)], ar_rsem.at[n, 0])
        part = jnp.sum(ya[n], axis=0)
        mid_a[n] = part
        za[n, mz] = part
        for who in z_ids:
            send(mid_a.at[n], za.at[n, mz], who, ar_ssem.at[n, 3], ar_rsem.at[n, 3])

    def sum_end(n):
        wait_for(za.at[n, pl.ds(0, NZ - 1)], ar_rsem.at[n, 3])
        wait_for(yb.at[n, pl.ds(0, NY - 1)], ar_rsem.at[n, 2])
        return jnp.concatenate([jnp.sum(za[n], axis=0), jnp.sum(yb[n], axis=0)], axis=0)

    def scalars_start(n, one, two):
        sc_send[n, pl.ds(0, 1), :] = one
        sc_send[n, pl.ds(1, 1), :] = two
        sy[n, my, pl.ds(0, 1), :] = one
        sy[n, my, pl.ds(1, 1), :] = two
        for who in y_ids:
            send(sc_send.at[n], sy.at[n, my], who, sc_ssem.at[n, 0], sc_rsem.at[n, 0])

    def scalars_middle(n):
        wait_for(sy.at[n, pl.ds(0, NY - 1)], sc_rsem.at[n, 0])
        part = jnp.sum(sy[n], axis=0)
        sc_mid[n] = part
        sz[n, mz] = part
        for who in z_ids:
            send(sc_mid.at[n], sz.at[n, mz], who, sc_ssem.at[n, 1], sc_rsem.at[n, 1])

    def response_start(n, packed):
        row = jnp.sum(packed * packed, axis=0, keepdims=True)
        rs_send[n] = row
        rs_buf[n, ms] = row
        for p in s_nums:
            send(rs_send.at[n], rs_buf.at[n, ms], {"sensor": p}, rs_ssem.at[n], rs_rsem.at[n])

    def step_size(n):
        wait_for(sz.at[n, pl.ds(0, NZ - 1)], sc_rsem.at[n, 1])
        wait_for(rs_buf.at[n, pl.ds(0, NSEN - 1)], rs_rsem.at[n])
        sums = jnp.sum(sz[n], axis=0)
        total = jnp.sum(sums, axis=1, keepdims=True)
        response = jnp.sum(jnp.sum(rs_buf[n], axis=0), axis=1, keepdims=True)
        return total[0:1] / (response + total[1:2] + TINY)

    def scatter_start(n):
        rs_in[n, ms] = gp[n, ms]
        for p in s_nums:
            send(gp.at[n, p], rs_in.at[n, ms], {"sensor": p}, gr_ssem.at[n, 0], gr_rsem.at[n, 0])

    def scatter_end(n):
        wait_for(rs_in.at[n, pl.ds(0, NSEN - 1)], gr_rsem.at[n, 0])
        return jnp.sum(rs_in[n], axis=0)

    def gather(n, piece):
        b_s[1 + n] = piece
        g_s[n, ms] = piece
        for p in s_nums:
            send(b_s.at[1 + n], g_s.at[n, ms], {"sensor": p}, gr_ssem.at[n, 1], gr_rsem.at[n, 1])
        wait_for(g_s.at[n, pl.ds(0, NSEN - 1)], gr_rsem.at[n, 1])
        send(g_s.at[n, pl.ds(8, 8)], gh_n.at[n], nxt_id, gh_ssem.at[n, 0], gh_rsem.at[n, 0])
        send(g_s.at[n, pl.ds(0, 8)], gh_s.at[n], prv_id, gh_ssem.at[n, 1], gh_rsem.at[n, 1])
        return g_s[n, 0:8].reshape(NT, ROW), g_s[n, 8:16].reshape(NT, ROW)

    def halo(n):
        wait_for(gh_n.at[n], gh_rsem.at[n, 0])
        wait_for(gh_s.at[n], gh_rsem.at[n, 1])
        return gh_n[n].reshape(NT, ROW), gh_s[n].reshape(NT, ROW)

    def jumps(dst, above, first, second, below):
        rows = (first, second)
        for r in range(2):
            dst[r] = jnp.where(linked[0][r], pltpu.roll(rows[r], ROW - 1, 1) - rows[r], 0.0)
            dst[2 + r] = jnp.where(linked[1][r], pltpu.roll(rows[r], 1, 1) - rows[r], 0.0)
            north = above if r == 0 else first
            south = second if r == 0 else below
            dst[4 + r] = jnp.where(linked[2][r], north - rows[r], 0.0)
            dst[6 + r] = jnp.where(linked[3][r], south - rows[r], 0.0)

    def squares(refs):
        total = jnp.zeros((1, ROW), F32)
        for value in refs:
            total = total + jnp.sum(value * value, axis=0, keepdims=True)
        return total

    def divergence(v):
        for r in range(2):
            from_south = v[5] if r == 0 else v[9]
            from_north = v[8] if r == 0 else v[6]
            total = jnp.where(linked[1][r], pltpu.roll(v[r], 1, 1), 0.0)
            total = total + jnp.where(linked[0][r], pltpu.roll(v[2 + r], ROW - 1, 1), 0.0)
            total = total + jnp.where(linked[3][r], from_south, 0.0)
            total = total + jnp.where(linked[2][r], from_north, 0.0)
            for k in range(4):
                total = total - jnp.where(linked[k][r], v[2 * k + r], 0.0)
            dt_s[8 * r : 8 * r + 8] = total.reshape(8, 8, ROW)

    first_sum = forward(x0_ref[...], True)
    pl.semaphore_wait(barrier, len(everyone))
    sum_start(0, first_sum)
    send(x0_ref.at[:, pl.ds(ROW, ROW)], h_n.at[pl.ds(0, 64)], nxt_id, h_ssem.at[0], h_rsem.at[0])
    send(m0_ref.at[3, :, pl.ds(ROW, ROW)], h_n.at[pl.ds(64, 64)], nxt_id, h_ssem.at[0], h_rsem.at[0])
    send(thr_s.at[1], h_n.at[pl.ds(128, 8)], nxt_id, h_ssem.at[0], h_rsem.at[0])
    send(x0_ref.at[:, pl.ds(0, ROW)], h_s.at[pl.ds(0, 64)], prv_id, h_ssem.at[1], h_rsem.at[1])
    send(m0_ref.at[2, :, pl.ds(0, ROW)], h_s.at[pl.ds(64, 64)], prv_id, h_ssem.at[1], h_rsem.at[1])
    send(thr_s.at[0], h_s.at[pl.ds(128, 8)], prv_id, h_ssem.at[1], h_rsem.at[1])
    sum_middle(0)
    wait_for(h_n, h_rsem.at[0])
    wait_for(h_s, h_rsem.at[1])
    start = [m0_ref[k, :, r * ROW : (r + 1) * ROW] for k in range(4) for r in range(2)]
    start = start + [h_n[64:128], h_s[64:128]]
    divergence(start)
    jumps(jump_s, h_n[0:64], x0_ref[:, 0:ROW], x0_ref[:, ROW:], h_s[0:64])
    observed = jnp.concatenate([obs_ref[0:32], obs_ref[32:64]], axis=1)
    misfit = sum_end(0) - observed

    adjoint(misfit, gp.at[0])
    scatter_start(0)
    piece = scatter_end(0)
    b_s[0] = piece
    grad_a, grad_b = gather(0, piece + dt_s[ms])
    part = forward(jnp.concatenate([grad_a, grad_b], axis=1), False)
    sum_start(1, part)
    above, below = halo(0)
    grad_a = g_s[0, 0:8].reshape(NT, ROW)
    grad_b = g_s[0, 8:16].reshape(NT, ROW)
    jumps(gj_s, above, grad_a, grad_b, below)
    scalars_start(0, squares([grad_a, grad_b]), squares([gj_s[i] for i in range(8)]))
    sum_middle(1)
    scalars_middle(0)
    response = sum_end(1)
    response_start(0, response)
    adjoint(response, gp.at[1])
    scatter_start(1)
    size = step_size(0)
    penalty = []
    thresholds = [thr_s[0, 0:1], thr_s[1, 0:1], h_n[128:129], h_s[128:129]]
    for i in range(10):
        if i < 8:
            moved = jump_s[i] - size * gj_s[i]
            limit = thresholds[i % 2]
            held = m0_ref[i // 2, :, (i % 2) * ROW : (i % 2 + 1) * ROW]
            jump_s[i] = moved
        else:
            source = 4 if i == 8 else 7
            moved = -jump_s[source]
            limit = thresholds[i - 6]
            held = h_n[64:128] if i == 8 else h_s[64:128]
        shifted = moved + held
        shrunk = jnp.maximum(shifted - limit, 0.0) - jnp.maximum(-shifted - limit, 0.0)
        rest = shifted - shrunk
        if i < 8:
            mult_s[i] = rest
        penalty.append(moved - shrunk + rest)
    divergence(penalty)
    est_ref[:, 0:ROW] = x0_ref[:, 0:ROW] - size * g_s[0, 0:8].reshape(NT, ROW)
    est_ref[:, ROW:] = x0_ref[:, ROW:] - size * g_s[0, 8:16].reshape(NT, ROW)

    piece = b_s[0] - size * scatter_end(1)
    grad_a, grad_b = gather(1, piece + dt_s[ms])
    part = forward(jnp.concatenate([grad_a, grad_b], axis=1), False)
    sum_start(2, part)
    above, below = halo(1)
    grad_a = g_s[1, 0:8].reshape(NT, ROW)
    grad_b = g_s[1, 8:16].reshape(NT, ROW)
    jumps(gj_s, above, grad_a, grad_b, below)
    scalars_start(1, squares([grad_a, grad_b]), squares([gj_s[i] for i in range(8)]))
    sum_middle(2)
    scalars_middle(1)
    response_start(1, sum_end(2))
    size = step_size(1)
    est_ref[:, 0:ROW] = est_ref[:, 0:ROW] - size * g_s[1, 0:8].reshape(NT, ROW)
    est_ref[:, ROW:] = est_ref[:, ROW:] - size * g_s[1, 8:16].reshape(NT, ROW)
    for i in range(8):
        shifted = jump_s[i] - size * gj_s[i] + mult_s[i]
        limit = thresholds[i % 2]
        shrunk = jnp.maximum(shifted - limit, 0.0) - jnp.maximum(-shifted - limit, 0.0)
        k, r = i // 2, i % 2
        aux_ref[k, :, r * ROW : (r + 1) * ROW] = shrunk
        mul_ref[k, :, r * ROW : (r + 1) * ROW] = shifted - shrunk

    wait_for(h_n, h_ssem.at[0])
    wait_for(h_s, h_ssem.at[1])
    for n in range(3):
        wait_for(ya.at[n, pl.ds(0, NY - 1)], ar_ssem.at[n, 0])
        wait_for(zb.at[n, pl.ds(0, NZ - 1)], ar_ssem.at[n, 1])
        wait_for(yb.at[n, pl.ds(0, NY - 1)], ar_ssem.at[n, 2])
        wait_for(za.at[n, pl.ds(0, NZ - 1)], ar_ssem.at[n, 3])
    for n in range(2):
        wait_for(sy.at[n, pl.ds(0, NY - 1)], sc_ssem.at[n, 0])
        wait_for(sz.at[n, pl.ds(0, NZ - 1)], sc_ssem.at[n, 1])
        wait_for(rs_buf.at[n, pl.ds(0, NSEN - 1)], rs_ssem.at[n])
        wait_for(rs_in.at[n, pl.ds(0, NSEN - 1)], gr_ssem.at[n, 0])
        wait_for(g_s.at[n, pl.ds(0, NSEN - 1)], gr_ssem.at[n, 1])
        wait_for(gh_n.at[n], gh_ssem.at[n, 0])
        wait_for(gh_s.at[n], gh_ssem.at[n, 1])


def per_device(kernel, observed, start_model, start_multiplier, neighbours, tile, weight):
    vmem = pl.BlockSpec(memory_space=pltpu.VMEM)
    scratch = lambda *shape, dtype=F32: pltpu.VMEM(shape, dtype)
    dma = lambda *shape: pltpu.SemaphoreType.DMA(shape)
    analysis, back, synthesis, closing = (jnp.asarray(t) for t in tables())
    return pl.pallas_call(
        body,
        out_shape=(
            jax.ShapeDtypeStruct((NT, 256), F32),
            jax.ShapeDtypeStruct((4, NT, 256), F32),
            jax.ShapeDtypeStruct((4, NT, 256), F32),
        ),
        in_specs=[pl.BlockSpec(memory_space=pl.ANY)] + [vmem] * 10,
        out_specs=(vmem, vmem, vmem),
        scratch_shapes=[
            scratch(NF, 128, 256, dtype=BF16),
            scratch(ROWS, 256),
            scratch(ROWS, ROW),
            scratch(ROWS, ROW),
            scratch(ROWS, 256),
            scratch(3, 32, ROW),
            scratch(3, NY, 16, ROW),
            scratch(3, NZ, 16, ROW),
            scratch(3, NZ, 16, ROW),
            scratch(3, NY, 16, ROW),
            scratch(3, 16, ROW),
            scratch(3, 16, ROW),
            scratch(2, 2, ROW),
            scratch(2, 2, ROW),
            scratch(2, NY, 2, ROW),
            scratch(2, NZ, 2, ROW),
            scratch(2, 1, ROW),
            scratch(2, NSEN, 1, ROW),
            scratch(2, 16, 8, ROW),
            scratch(2, NSEN, 8, ROW),
            scratch(2, 16, 8, ROW),
            scratch(3, 8, ROW),
            scratch(16, 8, ROW),
            scratch(2, 8, ROW),
            scratch(136, ROW),
            scratch(136, ROW),
            scratch(2, 8, 8, ROW),
            scratch(2, 8, 8, ROW),
            scratch(8, NT, ROW),
            scratch(8, NT, ROW),
            scratch(8, NT, ROW),
            dma(2, 4),
            dma(2),
            dma(2),
            dma(3, 4),
            dma(3, 4),
            dma(2, 2),
            dma(2, 2),
            dma(2),
            dma(2),
            dma(2, 2),
            dma(2, 2),
            dma(2, 2),
            dma(2, 2),
        ],
        compiler_params=pltpu.CompilerParams(
            collective_id=0, has_side_effects=True, vmem_limit_bytes=48 * 1024 * 1024
        ),
        name="inversion",
    )(
        kernel, observed, start_model, start_multiplier, neighbours, tile.reshape(1, 256),
        weight.reshape(1, 64), analysis, back, synthesis, closing,
    )


def solution(mesh):
    split_mesh = Mesh(mesh.devices.reshape(NY, NZ, NSEN), ("y", "zh", "sensor"))
    cells = ("y", "zh")
    in_specs = (
        P(None, None, "sensor", cells),
        P(None, "sensor"),
        P(None, cells),
        P(None, None, cells),
        P(None, cells),
        P(cells),
        P(),
    )
    out_specs = (P(None, cells), P(None, None, cells), P(None, None, cells))
    return jax.shard_map(
        per_device, mesh=split_mesh, in_specs=in_specs, out_specs=out_specs, check_vma=False
    )
```

```python
import functools

import jax
import jax.numpy as jnp
import numpy as np
from jax import lax
from jax.experimental import pallas as pl
from jax.experimental.pallas import tpu as pltpu
from jax.sharding import Mesh
from jax.sharding import PartitionSpec as P

NT = 64
NF = 65
ROW = 128
NY = 8
NZ = 4
NSEN = 16
ROWS = 144
SHRINK_SCALE = 0.4
TINY = 1e-06
UNROLL = 16
MAIN_VMEM = 67043328
F32 = jnp.float32
BF16 = jnp.bfloat16
MESH = pl.DeviceIdType.MESH
Y_ORDER = (4, 3, 5, 2, 6, 1, 7)
Z_ORDER = (2, 1, 3)


def high_low(table):
    high = table.astype(BF16)
    low = (table - high.astype(np.float32)).astype(BF16)
    return high, low


def tables():
    freq = np.arange(NF)[:, None]
    time = np.arange(NT)[None, :]
    phase = 2.0 * np.pi * (freq * time % (2 * NT)) / (2 * NT)
    cosine, sine = np.cos(phase), np.sin(phase)
    weight = np.where((freq == 0) | (freq == NF - 1), 1.0, 2.0) / (2 * NT)
    wcos, wsin = cosine * weight, sine * weight

    def interleaved(even, odd):
        out = np.zeros((ROWS, NT), np.float32)
        out[0 : 2 * NF : 2] = even
        out[1 : 2 * NF : 2] = odd
        return out

    analysis = interleaved(cosine, -sine)
    back = np.concatenate([interleaved(wcos, -wsin), interleaved(-wsin, -wcos)], axis=0)
    synthesis = np.concatenate([interleaved(wcos, -wsin).T, interleaved(wsin, wcos).T], axis=0)
    ah, al = high_low(analysis)
    bh, bl = high_low(back)
    sh, sl = high_low(synthesis)
    ch, cl = high_low(analysis.T)
    return (
        np.concatenate([ah, al, ah, al], axis=1),
        np.concatenate([bh, bl, bh, bl], axis=1),
        np.stack([sh, sl]),
        np.stack([ch, cl]),
    )


def split(value):
    high = value.astype(BF16)
    return high, (value - high.astype(F32)).astype(BF16)


def dot(left, right, dims=((1,), (0,))):
    return lax.dot_general(left, right, (dims, ((), ())), preferred_element_type=F32)


def dot3(table_ref, value):
    high, low = split(value)
    th = table_ref[0]
    return dot(th, high) + dot(th, low) + dot(table_ref[1], high)


def stacked(value):
    high, low = split(value)
    return jnp.concatenate([high, high, low, low], axis=0)


def body(
    k_hbm, obs_hbm, x0_hbm, m0_hbm, nb_hbm, tile_hbm, w_hbm, tf_hbm, ta_hbm, ti_hbm, ts_hbm,
    est_hbm, aux_hbm, mul_hbm,
    kv, est_ref, aux_ref, mul_ref, obs_ref, x0_ref, m0_ref, nb_ref, tile_ref, w_ref, tf_ref, ta_ref, ti_ref, ts_ref, m_s, ab_s, l_s, q_s,
    send1, ya, zb, za, yb, mid_a, mid_b,
    sc_send, sc_mid, sy, sz, rs_send, rs_buf,
    gp, rs_in, g_s, b_s, dt_s, thr_s, h_n, h_s, gh_n, gh_s,
    jump_s, gj_s, mult_s,
    k_sem, in_sem, out_sem, h_ssem, h_rsem, ar_ssem, ar_rsem, sc_ssem, sc_rsem, rs_ssem, rs_rsem, gr_ssem, gr_rsem,
    gh_ssem, gh_rsem,
):
    my = lax.axis_index("y")
    mz = lax.axis_index("zh")
    ms = lax.axis_index("sensor")
    cell = my * NZ + mz
    nxt = (cell + 1) % (NY * NZ)
    prv = (cell + NY * NZ - 1) % (NY * NZ)
    nxt_id = {"y": nxt // NZ, "zh": nxt % NZ}
    prv_id = {"y": prv // NZ, "zh": prv % NZ}
    y_ids = [{"y": (my + j) % NY} for j in Y_ORDER]
    z_ids = [{"zh": (mz + j) % NZ} for j in Z_ORDER]
    s_nums = [(ms + j) % NSEN for j in (7, 9, 6, 10, 5, 11, 4, 12, 3, 13, 8, 2, 14, 1, 15)]

    def load(i):
        src, dst = loads[i]
        return pltpu.make_async_copy(src, dst, in_sem.at[i])

    loads = (
        (x0_hbm, x0_ref), (tf_hbm, tf_ref), (ti_hbm, ti_ref), (w_hbm, w_ref), (tile_hbm, tile_ref),
        (nb_hbm, nb_ref), (m0_hbm, m0_ref), (obs_hbm, obs_ref), (ta_hbm, ta_ref), (ts_hbm, ts_ref),
    )
    load(0).start()
    load(1).start()

    barrier = pltpu.get_barrier_semaphore()
    everyone = y_ids + z_ids + [{"sensor": p} for p in s_nums] + [nxt_id, prv_id]
    for who in everyone:
        pl.semaphore_signal(barrier, inc=1, device_id=who, device_id_type=MESH)

    bounds = (0, 16, 32, 48, 65)

    def k_copy(plane, q):
        lo, hi = bounds[q], bounds[q + 1]
        return pltpu.make_async_copy(
            k_hbm.at[plane, pl.ds(lo, hi - lo)],
            kv.at[pl.ds(lo, hi - lo), pl.ds(64 * plane, 64)],
            k_sem.at[plane, q],
        )

    for q in range(4):
        for plane in range(2):
            k_copy(plane, q).start()
    for i in range(2, 10):
        load(i).start()

    def send(src, dst, who, ssem, rsem):
        pltpu.make_async_remote_copy(
            src_ref=src, dst_ref=dst, send_sem=ssem, recv_sem=rsem, device_id=who,
            device_id_type=MESH,
        ).start()

    def wait_for(view, sem):
        pltpu.make_async_copy(view, view, sem).wait()

    lane = lax.broadcasted_iota(jnp.int32, (1, ROW), 1)
    left_half = lane < 64

    def prepare():
        for i in (3, 4, 5):
            load(i).wait()
        column = jnp.sum(
            jnp.where(
                lax.broadcasted_iota(jnp.int32, (64, 64), 0)
                == lax.broadcasted_iota(jnp.int32, (64, 64), 1),
                jnp.broadcast_to(w_ref[...], (64, 64)), 0.0,
            ),
            axis=1, keepdims=True,
        )
        labels = lax.broadcasted_iota(jnp.int32, (64, 2 * ROW), 0)
        threshold = SHRINK_SCALE * jnp.sum(
            jnp.where(labels == tile_ref[...], column, 0.0), axis=0, keepdims=True
        )
        thr_s[0] = jnp.broadcast_to(threshold[:, :ROW], (8, ROW))
        thr_s[1] = jnp.broadcast_to(threshold[:, ROW:], (8, ROW))

    group_row = lax.broadcasted_iota(jnp.int32, (8, ROW), 0) // 2

    def forward(field, first):
        m_s[...] = dot(tf_ref[...], stacked(field))

        def step(i, carry):
            moved = m_s[pl.ds(pl.multiple_of(8 * i, 8), 8), :].astype(BF16)
            weights = kv[pl.ds(4 * i, 4)].reshape(512, 256)
            out = dot(moved, weights, ((1,), (1,)))
            kept = out[:, 0:ROW]
            for j in range(1, 4):
                kept = jnp.where(group_row == j, out[:, j * ROW : (j + 1) * ROW], kept)
            ab_s[pl.ds(pl.multiple_of(8 * i, 8), 8), :] = kept
            return carry

        if first:
            for q in range(4):
                k_copy(0, q).wait()
                k_copy(1, q).wait()
                lax.fori_loop(4 * q, 4 * q + 4, step, 0, unroll=4)
        else:
            lax.fori_loop(0, 16, step, 0, unroll=UNROLL)
        tail = m_s[128:136, :].astype(BF16)
        ab_s[128:136, :] = dot(tail, kv[64], ((1,), (1,)))
        ab_s[136:144, :] = jnp.zeros((8, ROW), F32)
        if first:
            load(2).wait()
        out = dot3(ti_ref, ab_s[...])
        low = out[0:32] - pltpu.roll(out[64:96], 64, 1)
        high = pltpu.roll(out[32:64], 64, 1) - out[96:128]
        return jnp.where(left_half, low, high)

    def adjoint(packed, dst):
        turned = pltpu.roll(packed, 64, 1)
        doubled = jnp.concatenate(
            [jnp.where(left_half, packed, turned), jnp.where(left_half, turned, packed)], axis=0
        )
        out = dot(ta_ref[...], stacked(doubled))
        l_s[...] = jnp.where(left_half, out[:ROWS], out[ROWS:])

        def step(i, carry):
            rows = l_s[pl.ds(pl.multiple_of(8 * i, 8), 8), :]
            moved = jnp.concatenate(
                [jnp.where(group_row == j, rows, 0.0) for j in range(4)], axis=1
            ).astype(BF16)
            weights = kv[pl.ds(4 * i, 4)].reshape(512, 256)
            q_s[pl.ds(pl.multiple_of(8 * i, 8), 8), :] = dot(moved, weights)
            return carry

        lax.fori_loop(0, 16, step, 0, unroll=UNROLL)
        q_s[128:136, :] = dot(l_s[128:136, :].astype(BF16), kv[64])
        q_s[136:144, :] = jnp.zeros((8, 256), F32)
        out = dot3(ts_ref, q_s[...])
        dst[0:8] = out[:, :ROW].reshape(8, 8, ROW)
        dst[8:16] = out[:, ROW:].reshape(8, 8, ROW)

    def sum_start(n, packed):
        send1[n] = packed
        ya[n, my] = packed[0:16]
        zb[n, mz] = packed[16:32]
        for who in y_ids:
            send(send1.at[n, pl.ds(0, 16)], ya.at[n, my], who, ar_ssem.at[n, 0], ar_rsem.at[n, 0])
        for who in z_ids:
            send(send1.at[n, pl.ds(16, 16)], zb.at[n, mz], who, ar_ssem.at[n, 1], ar_rsem.at[n, 1])

    def sum_middle(n):
        wait_for(zb.at[n, pl.ds(0, NZ - 1)], ar_rsem.at[n, 1])
        part = jnp.sum(zb[n], axis=0)
        mid_b[n] = part
        yb[n, my] = part
        for who in y_ids:
            send(mid_b.at[n], yb.at[n, my], who, ar_ssem.at[n, 2], ar_rsem.at[n, 2])
        wait_for(ya.at[n, pl.ds(0, NY - 1)], ar_rsem.at[n, 0])
        part = jnp.sum(ya[n], axis=0)
        mid_a[n] = part
        za[n, mz] = part
        for who in z_ids:
            send(mid_a.at[n], za.at[n, mz], who, ar_ssem.at[n, 3], ar_rsem.at[n, 3])

    def sum_end(n):
        wait_for(za.at[n, pl.ds(0, NZ - 1)], ar_rsem.at[n, 3])
        wait_for(yb.at[n, pl.ds(0, NY - 1)], ar_rsem.at[n, 2])
        return jnp.concatenate([jnp.sum(za[n], axis=0), jnp.sum(yb[n], axis=0)], axis=0)

    def scalars_start(n, one, two):
        sc_send[n, pl.ds(0, 1), :] = one
        sc_send[n, pl.ds(1, 1), :] = two
        sy[n, my, pl.ds(0, 1), :] = one
        sy[n, my, pl.ds(1, 1), :] = two
        for who in y_ids:
            send(sc_send.at[n], sy.at[n, my], who, sc_ssem.at[n, 0], sc_rsem.at[n, 0])

    def scalars_middle(n):
        wait_for(sy.at[n, pl.ds(0, NY - 1)], sc_rsem.at[n, 0])
        part = jnp.sum(sy[n], axis=0)
        sc_mid[n] = part
        sz[n, mz] = part
        for who in z_ids:
            send(sc_mid.at[n], sz.at[n, mz], who, sc_ssem.at[n, 1], sc_rsem.at[n, 1])

    def response_start(n, packed):
        row = jnp.sum(packed * packed, axis=0, keepdims=True)
        rs_send[n] = row
        rs_buf[n, ms] = row
        for p in s_nums:
            send(rs_send.at[n], rs_buf.at[n, ms], {"sensor": p}, rs_ssem.at[n], rs_rsem.at[n])

    def step_size(n):
        wait_for(sz.at[n, pl.ds(0, NZ - 1)], sc_rsem.at[n, 1])
        wait_for(rs_buf.at[n, pl.ds(0, NSEN - 1)], rs_rsem.at[n])
        sums = jnp.sum(sz[n], axis=0)
        total = jnp.sum(sums, axis=1, keepdims=True)
        response = jnp.sum(jnp.sum(rs_buf[n], axis=0), axis=1, keepdims=True)
        return total[0:1] / (response + total[1:2] + TINY)

    def scatter_start(n):
        rs_in[n, ms] = gp[n, ms]
        for p in s_nums:
            send(gp.at[n, p], rs_in.at[n, ms], {"sensor": p}, gr_ssem.at[n, 0], gr_rsem.at[n, 0])

    def scatter_end(n):
        wait_for(rs_in.at[n, pl.ds(0, NSEN - 1)], gr_rsem.at[n, 0])
        return jnp.sum(rs_in[n], axis=0)

    def gather(n, piece):
        b_s[1 + n] = piece
        g_s[n, ms] = piece
        for p in s_nums:
            send(b_s.at[1 + n], g_s.at[n, ms], {"sensor": p}, gr_ssem.at[n, 1], gr_rsem.at[n, 1])
        wait_for(g_s.at[n, pl.ds(0, NSEN - 1)], gr_rsem.at[n, 1])
        send(g_s.at[n, pl.ds(8, 8)], gh_n.at[n], nxt_id, gh_ssem.at[n, 0], gh_rsem.at[n, 0])
        send(g_s.at[n, pl.ds(0, 8)], gh_s.at[n], prv_id, gh_ssem.at[n, 1], gh_rsem.at[n, 1])
        return g_s[n, 0:8].reshape(NT, ROW), g_s[n, 8:16].reshape(NT, ROW)

    def halo(n):
        wait_for(gh_n.at[n], gh_rsem.at[n, 0])
        wait_for(gh_s.at[n], gh_rsem.at[n, 1])
        return gh_n[n].reshape(NT, ROW), gh_s[n].reshape(NT, ROW)

    def jumps(dst, above, first, second, below):
        rows = (first, second)
        for r in range(2):
            dst[r] = jnp.where(linked[0][r], pltpu.roll(rows[r], ROW - 1, 1) - rows[r], 0.0)
            dst[2 + r] = jnp.where(linked[1][r], pltpu.roll(rows[r], 1, 1) - rows[r], 0.0)
            north = above if r == 0 else first
            south = second if r == 0 else below
            dst[4 + r] = jnp.where(linked[2][r], north - rows[r], 0.0)
            dst[6 + r] = jnp.where(linked[3][r], south - rows[r], 0.0)

    def squares(refs):
        total = jnp.zeros((1, ROW), F32)
        for value in refs:
            total = total + jnp.sum(value * value, axis=0, keepdims=True)
        return total

    def divergence(v):
        for r in range(2):
            from_south = v[5] if r == 0 else v[9]
            from_north = v[8] if r == 0 else v[6]
            total = jnp.where(linked[1][r], pltpu.roll(v[r], 1, 1), 0.0)
            total = total + jnp.where(linked[0][r], pltpu.roll(v[2 + r], ROW - 1, 1), 0.0)
            total = total + jnp.where(linked[3][r], from_south, 0.0)
            total = total + jnp.where(linked[2][r], from_north, 0.0)
            for k in range(4):
                total = total - jnp.where(linked[k][r], v[2 * k + r], 0.0)
            dt_s[8 * r : 8 * r + 8] = total.reshape(8, 8, ROW)

    load(0).wait()
    load(1).wait()
    first_sum = forward(x0_ref[...], True)
    prepare()
    own = cell * (2 * ROW) + lax.broadcasted_iota(jnp.int32, (1, 2 * ROW), 1)
    linked = [[None, None] for _ in range(4)]
    for k in range(4):
        both = jnp.where(nb_ref[pl.ds(k, 1), :] != own, 1.0, 0.0)
        linked[k][0] = both[:, :ROW] > 0.5
        linked[k][1] = both[:, ROW:] > 0.5
    load(6).wait()
    pl.semaphore_wait(barrier, len(everyone))
    sum_start(0, first_sum)
    send(x0_ref.at[:, pl.ds(ROW, ROW)], h_n.at[pl.ds(0, 64)], nxt_id, h_ssem.at[0], h_rsem.at[0])
    send(m0_ref.at[3, :, pl.ds(ROW, ROW)], h_n.at[pl.ds(64, 64)], nxt_id, h_ssem.at[0], h_rsem.at[0])
    send(thr_s.at[1], h_n.at[pl.ds(128, 8)], nxt_id, h_ssem.at[0], h_rsem.at[0])
    send(x0_ref.at[:, pl.ds(0, ROW)], h_s.at[pl.ds(0, 64)], prv_id, h_ssem.at[1], h_rsem.at[1])
    send(m0_ref.at[2, :, pl.ds(0, ROW)], h_s.at[pl.ds(64, 64)], prv_id, h_ssem.at[1], h_rsem.at[1])
    send(thr_s.at[0], h_s.at[pl.ds(128, 8)], prv_id, h_ssem.at[1], h_rsem.at[1])
    sum_middle(0)
    wait_for(h_n, h_rsem.at[0])
    wait_for(h_s, h_rsem.at[1])
    start = [m0_ref[k, :, r * ROW : (r + 1) * ROW] for k in range(4) for r in range(2)]
    start = start + [h_n[64:128], h_s[64:128]]
    divergence(start)
    jumps(jump_s, h_n[0:64], x0_ref[:, 0:ROW], x0_ref[:, ROW:], h_s[0:64])
    for i in (7, 8, 9):
        load(i).wait()
    observed = jnp.concatenate([obs_ref[0:32], obs_ref[32:64]], axis=1)
    misfit = sum_end(0) - observed

    adjoint(misfit, gp.at[0])
    scatter_start(0)
    piece = scatter_end(0)
    b_s[0] = piece
    grad_a, grad_b = gather(0, piece + dt_s[ms])
    part = forward(jnp.concatenate([grad_a, grad_b], axis=1), False)
    sum_start(1, part)
    above, below = halo(0)
    grad_a = g_s[0, 0:8].reshape(NT, ROW)
    grad_b = g_s[0, 8:16].reshape(NT, ROW)
    jumps(gj_s, above, grad_a, grad_b, below)
    scalars_start(0, squares([grad_a, grad_b]), squares([gj_s[i] for i in range(8)]))
    sum_middle(1)
    scalars_middle(0)
    response = sum_end(1)
    response_start(0, response)
    adjoint(response, gp.at[1])
    scatter_start(1)
    size = step_size(0)
    penalty = []
    thresholds = [thr_s[0, 0:1], thr_s[1, 0:1], h_n[128:129], h_s[128:129]]
    for i in range(10):
        if i < 8:
            moved = jump_s[i] - size * gj_s[i]
            limit = thresholds[i % 2]
            held = m0_ref[i // 2, :, (i % 2) * ROW : (i % 2 + 1) * ROW]
            jump_s[i] = moved
        else:
            source = 4 if i == 8 else 7
            moved = -jump_s[source]
            limit = thresholds[i - 6]
            held = h_n[64:128] if i == 8 else h_s[64:128]
        shifted = moved + held
        shrunk = jnp.maximum(shifted - limit, 0.0) - jnp.maximum(-shifted - limit, 0.0)
        rest = shifted - shrunk
        if i < 8:
            mult_s[i] = rest
        penalty.append(moved - shrunk + rest)
    divergence(penalty)
    est_ref[:, 0:ROW] = x0_ref[:, 0:ROW] - size * g_s[0, 0:8].reshape(NT, ROW)
    est_ref[:, ROW:] = x0_ref[:, ROW:] - size * g_s[0, 8:16].reshape(NT, ROW)

    piece = b_s[0] - size * scatter_end(1)
    grad_a, grad_b = gather(1, piece + dt_s[ms])
    part = forward(jnp.concatenate([grad_a, grad_b], axis=1), False)
    sum_start(2, part)
    above, below = halo(1)
    grad_a = g_s[1, 0:8].reshape(NT, ROW)
    grad_b = g_s[1, 8:16].reshape(NT, ROW)
    jumps(gj_s, above, grad_a, grad_b, below)
    scalars_start(1, squares([grad_a, grad_b]), squares([gj_s[i] for i in range(8)]))
    sum_middle(2)
    scalars_middle(1)
    response_start(1, sum_end(2))
    size = step_size(1)
    est_ref[:, 0:ROW] = est_ref[:, 0:ROW] - size * g_s[1, 0:8].reshape(NT, ROW)
    est_ref[:, ROW:] = est_ref[:, ROW:] - size * g_s[1, 8:16].reshape(NT, ROW)
    outs = [pltpu.make_async_copy(est_ref, est_hbm, out_sem.at[8])]
    outs[0].start()
    for i in range(8):
        shifted = jump_s[i] - size * gj_s[i] + mult_s[i]
        limit = thresholds[i % 2]
        shrunk = jnp.maximum(shifted - limit, 0.0) - jnp.maximum(-shifted - limit, 0.0)
        k, r = i // 2, i % 2
        aux_ref[k, :, r * ROW : (r + 1) * ROW] = shrunk
        mul_ref[k, :, r * ROW : (r + 1) * ROW] = shifted - shrunk
        if r == 1:
            for n, (src, dst) in enumerate(((aux_ref, aux_hbm), (mul_ref, mul_hbm))):
                outs.append(pltpu.make_async_copy(src.at[k], dst.at[k], out_sem.at[4 * n + k]))
                outs[-1].start()

    for copy in outs:
        copy.wait()
    wait_for(h_n, h_ssem.at[0])
    wait_for(h_s, h_ssem.at[1])
    for n in range(3):
        wait_for(ya.at[n, pl.ds(0, NY - 1)], ar_ssem.at[n, 0])
        wait_for(zb.at[n, pl.ds(0, NZ - 1)], ar_ssem.at[n, 1])
        wait_for(yb.at[n, pl.ds(0, NY - 1)], ar_ssem.at[n, 2])
        wait_for(za.at[n, pl.ds(0, NZ - 1)], ar_ssem.at[n, 3])
    for n in range(2):
        wait_for(sy.at[n, pl.ds(0, NY - 1)], sc_ssem.at[n, 0])
        wait_for(sz.at[n, pl.ds(0, NZ - 1)], sc_ssem.at[n, 1])
        wait_for(rs_buf.at[n, pl.ds(0, NSEN - 1)], rs_ssem.at[n])
        wait_for(rs_in.at[n, pl.ds(0, NSEN - 1)], gr_ssem.at[n, 0])
        wait_for(g_s.at[n, pl.ds(0, NSEN - 1)], gr_ssem.at[n, 1])
        wait_for(gh_n.at[n], gh_ssem.at[n, 0])
        wait_for(gh_s.at[n], gh_ssem.at[n, 1])


def finish(est, aux, mul, est_out, aux_out, mul_out, est_v, aux_v, mul_v, sems):
    moves = ((aux, aux_v, aux_out), (mul, mul_v, mul_out), (est, est_v, est_out))
    arriving = [
        pltpu.make_async_copy(src, mid, sems.at[0, i]) for i, (src, mid, _) in enumerate(moves)
    ]
    leaving = [
        pltpu.make_async_copy(mid, dst, sems.at[1, i]) for i, (_, mid, dst) in enumerate(moves)
    ]
    for copy in arriving:
        copy.start()
    for first, second in zip(arriving, leaving):
        first.wait()
        second.start()
    for copy in leaving:
        copy.wait()


def per_device(kernel, observed, start_model, start_multiplier, neighbours, tile, weight):
    hbm = pl.BlockSpec(memory_space=pltpu.HBM)
    scratch = lambda *shape, dtype=F32: pltpu.VMEM(shape, dtype)
    dma = lambda *shape: pltpu.SemaphoreType.DMA(shape)
    analysis, back, synthesis, closing = (jnp.asarray(t) for t in tables())
    results = pl.pallas_call(
        body,
        out_shape=(
            jax.ShapeDtypeStruct((NT, 256), F32),
            jax.ShapeDtypeStruct((4, NT, 256), F32),
            jax.ShapeDtypeStruct((4, NT, 256), F32),
        ),
        in_specs=[hbm] * 11,
        out_specs=(hbm, hbm, hbm),
        scratch_shapes=[
            scratch(NF, 128, 256, dtype=BF16),
            scratch(NT, 256),
            scratch(4, NT, 256),
            scratch(4, NT, 256),
            scratch(NT, 64),
            scratch(NT, 256),
            scratch(4, NT, 256),
            scratch(4, 256, dtype=jnp.int32),
            scratch(1, 256, dtype=jnp.int32),
            scratch(1, 64),
            scratch(ROWS, 256, dtype=BF16),
            scratch(2 * ROWS, 256, dtype=BF16),
            scratch(2, 128, ROWS, dtype=BF16),
            scratch(2, NT, ROWS, dtype=BF16),
            scratch(ROWS, 256),
            scratch(ROWS, ROW),
            scratch(ROWS, ROW),
            scratch(ROWS, 256),
            scratch(3, 32, ROW),
            scratch(3, NY, 16, ROW),
            scratch(3, NZ, 16, ROW),
            scratch(3, NZ, 16, ROW),
            scratch(3, NY, 16, ROW),
            scratch(3, 16, ROW),
            scratch(3, 16, ROW),
            scratch(2, 2, ROW),
            scratch(2, 2, ROW),
            scratch(2, NY, 2, ROW),
            scratch(2, NZ, 2, ROW),
            scratch(2, 1, ROW),
            scratch(2, NSEN, 1, ROW),
            scratch(2, 16, 8, ROW),
            scratch(2, NSEN, 8, ROW),
            scratch(2, 16, 8, ROW),
            scratch(3, 8, ROW),
            scratch(16, 8, ROW),
            scratch(2, 8, ROW),
            scratch(136, ROW),
            scratch(136, ROW),
            scratch(2, 8, 8, ROW),
            scratch(2, 8, 8, ROW),
            scratch(8, NT, ROW),
            scratch(8, NT, ROW),
            scratch(8, NT, ROW),
            dma(2, 4),
            dma(10),
            dma(9),
            dma(2),
            dma(2),
            dma(3, 4),
            dma(3, 4),
            dma(2, 2),
            dma(2, 2),
            dma(2),
            dma(2),
            dma(2, 2),
            dma(2, 2),
            dma(2, 2),
            dma(2, 2),
        ],
        compiler_params=pltpu.CompilerParams(
            collective_id=0, has_side_effects=True, vmem_limit_bytes=MAIN_VMEM
        ),
        name="inversion",
    )(
        kernel, observed, start_model, start_multiplier, neighbours, tile.reshape(1, 256),
        weight.reshape(1, 64), analysis, back, synthesis, closing,
    )
    return pl.pallas_call(
        finish,
        out_shape=tuple(jax.ShapeDtypeStruct(r.shape, F32) for r in results),
        in_specs=[hbm] * 3,
        out_specs=(hbm, hbm, hbm),
        scratch_shapes=[pltpu.VMEM(r.shape, F32) for r in results] + [dma(2, 3)],
        compiler_params=pltpu.CompilerParams(vmem_limit_bytes=MAIN_VMEM),
        name="finish",
    )(*results)


def solution(mesh):
    split_mesh = Mesh(mesh.devices.reshape(NY, NZ, NSEN), ("y", "zh", "sensor"))
    cells = ("y", "zh")
    in_specs = (
        P(None, None, "sensor", cells),
        P(None, "sensor"),
        P(None, cells),
        P(None, None, cells),
        P(None, cells),
        P(cells),
        P(),
    )
    out_specs = (P(None, cells), P(None, None, cells), P(None, None, cells))
    return jax.shard_map(
        per_device, mesh=split_mesh, in_specs=in_specs, out_specs=out_specs, check_vma=False
    )
```

```python
import functools

import jax
import jax.numpy as jnp
import numpy as np
from jax import lax
from jax.experimental import pallas as pl
from jax.experimental.pallas import tpu as pltpu
from jax.sharding import Mesh
from jax.sharding import PartitionSpec as P

NT = 64
NF = 65
ROW = 128
NY = 8
NZ = 4
NSEN = 16
ROWS = 144
SHRINK_SCALE = 0.4
TINY = 1e-06
UNROLL = 16
MAIN_VMEM = 40 * 1024 * 1024
F32 = jnp.float32
BF16 = jnp.bfloat16
MESH = pl.DeviceIdType.MESH
Y_ORDER = (4, 3, 5, 2, 6, 1, 7)
Z_ORDER = (2, 1, 3)


def high_low(table):
    high = table.astype(BF16)
    low = (table - high.astype(np.float32)).astype(BF16)
    return high, low


def tables():
    freq = np.arange(NF)[:, None]
    time = np.arange(NT)[None, :]
    phase = 2.0 * np.pi * (freq * time % (2 * NT)) / (2 * NT)
    cosine, sine = np.cos(phase), np.sin(phase)
    weight = np.where((freq == 0) | (freq == NF - 1), 1.0, 2.0) / (2 * NT)
    wcos, wsin = cosine * weight, sine * weight

    def interleaved(even, odd):
        out = np.zeros((ROWS, NT), np.float32)
        out[0 : 2 * NF : 2] = even
        out[1 : 2 * NF : 2] = odd
        return out

    analysis = interleaved(cosine, -sine)
    back = np.concatenate([interleaved(wcos, -wsin), interleaved(-wsin, -wcos)], axis=0)
    synthesis = np.concatenate([interleaved(wcos, -wsin).T, interleaved(wsin, wcos).T], axis=0)
    ah, al = high_low(analysis)
    bh, bl = high_low(back)
    sh, sl = high_low(synthesis)
    ch, cl = high_low(analysis.T)
    return (
        np.concatenate([ah, al, ah, al], axis=1),
        np.concatenate([bh, bl, bh, bl], axis=1),
        np.stack([sh, sl]),
        np.stack([ch, cl]),
    )


def split(value):
    high = value.astype(BF16)
    return high, (value - high.astype(F32)).astype(BF16)


def dot(left, right, dims=((1,), (0,))):
    return lax.dot_general(left, right, (dims, ((), ())), preferred_element_type=F32)


def dot3(table_ref, value):
    high, low = split(value)
    th = table_ref[0]
    return dot(th, high) + dot(th, low) + dot(table_ref[1], high)


def stacked(value):
    high, low = split(value)
    return jnp.concatenate([high, high, low, low], axis=0)


def body(
    k_hbm, obs_hbm, x0_hbm, m0_hbm, nb_hbm, tile_hbm, w_hbm, tf_hbm, ta_hbm, ti_hbm, ts_hbm,
    est_ref, aux_ref, mul_ref,
    kv, obs_ref, x0_ref, m0_ref, nb_ref, tile_ref, w_ref, tf_ref, ta_ref, ti_ref, ts_ref, m_s, ab_s, l_s, q_s,
    send1, ya, zb, za, yb, mid_a, mid_b,
    sc_send, sc_mid, sy, sz, rs_send, rs_buf,
    gp, rs_in, g_s, b_s, dt_s, thr_s, h_m, h_t, hx_n, hx_s, gh_n, gh_s,
    jump_s, gj_s, mult_s,
    k_sem, in_sem, h_ssem, h_rsem, ar_ssem, ar_rsem, sc_ssem, sc_rsem, rs_ssem, rs_rsem, gr_ssem, gr_rsem,
    gh_ssem, gh_rsem,
):
    my = lax.axis_index("y")
    mz = lax.axis_index("zh")
    ms = lax.axis_index("sensor")
    cell = my * NZ + mz
    nxt = (cell + 1) % (NY * NZ)
    prv = (cell + NY * NZ - 1) % (NY * NZ)
    nxt_id = {"y": nxt // NZ, "zh": nxt % NZ}
    prv_id = {"y": prv // NZ, "zh": prv % NZ}
    y_ids = [{"y": (my + j) % NY} for j in Y_ORDER]
    z_ids = [{"zh": (mz + j) % NZ} for j in Z_ORDER]
    s_nums = [(ms + j) % NSEN for j in (7, 9, 6, 10, 5, 11, 4, 12, 3, 13, 8, 2, 14, 1, 15)]

    tb = ms % 8
    half = ms // 8
    edge = (cell + NY * NZ + 1 - 2 * half) % (NY * NZ)
    edge_id = {"y": edge // NZ, "zh": edge % NZ}

    def load(i):
        src, dst = loads[i]
        return pltpu.make_async_copy(src, dst, in_sem.at[i])

    loads = (
        (x0_hbm, x0_ref), (tf_hbm, tf_ref), (ti_hbm, ti_ref), (w_hbm, w_ref), (tile_hbm, tile_ref),
        (nb_hbm, nb_ref), (m0_hbm, m0_ref), (obs_hbm, obs_ref), (ta_hbm, ta_ref), (ts_hbm, ts_ref),
    )
    load(0).start()
    load(1).start()

    bounds = (0, 16, 32, 48, 65)

    def k_copy(plane, q):
        lo, hi = bounds[q], bounds[q + 1]
        return pltpu.make_async_copy(
            k_hbm.at[plane, pl.ds(lo, hi - lo)],
            kv.at[pl.ds(lo, hi - lo), pl.ds(64 * plane, 64)],
            k_sem.at[plane, q],
        )

    for q in range(4):
        for plane in range(2):
            k_copy(plane, q).start()
    barrier = pltpu.get_barrier_semaphore()
    everyone = y_ids + z_ids + [{"sensor": p} for p in s_nums] + [nxt_id, prv_id]
    for who in everyone:
        pl.semaphore_signal(barrier, inc=1, device_id=who, device_id_type=MESH)

    for i in range(2, 10):
        load(i).start()

    def send(src, dst, who, ssem, rsem):
        pltpu.make_async_remote_copy(
            src_ref=src, dst_ref=dst, send_sem=ssem, recv_sem=rsem, device_id=who,
            device_id_type=MESH,
        ).start()

    def wait_for(view, sem):
        pltpu.make_async_copy(view, view, sem).wait()

    lane = lax.broadcasted_iota(jnp.int32, (1, ROW), 1)
    left_half = lane < 64

    def prepare():
        for i in (3, 4, 5):
            load(i).wait()
        column = jnp.sum(
            jnp.where(
                lax.broadcasted_iota(jnp.int32, (64, 64), 0)
                == lax.broadcasted_iota(jnp.int32, (64, 64), 1),
                jnp.broadcast_to(w_ref[...], (64, 64)), 0.0,
            ),
            axis=1, keepdims=True,
        )
        labels = lax.broadcasted_iota(jnp.int32, (64, 2 * ROW), 0)
        threshold = SHRINK_SCALE * jnp.sum(
            jnp.where(labels == tile_ref[...], column, 0.0), axis=0, keepdims=True
        )
        thr_s[0] = jnp.broadcast_to(threshold[:, :ROW], (8, ROW))
        thr_s[1] = jnp.broadcast_to(threshold[:, ROW:], (8, ROW))

    group_row = lax.broadcasted_iota(jnp.int32, (8, ROW), 0) // 2

    def forward(field, first):
        m_s[...] = dot(tf_ref[...], stacked(field))

        def step(i, carry):
            moved = m_s[pl.ds(pl.multiple_of(8 * i, 8), 8), :].astype(BF16)
            weights = kv[pl.ds(4 * i, 4)].reshape(512, 256)
            out = dot(moved, weights, ((1,), (1,)))
            kept = out[:, 0:ROW]
            for j in range(1, 4):
                kept = jnp.where(group_row == j, out[:, j * ROW : (j + 1) * ROW], kept)
            ab_s[pl.ds(pl.multiple_of(8 * i, 8), 8), :] = kept
            return carry

        if first:
            for q in range(4):
                k_copy(0, q).wait()
                k_copy(1, q).wait()
                lax.fori_loop(4 * q, 4 * q + 4, step, 0, unroll=4)
        else:
            lax.fori_loop(0, 16, step, 0, unroll=UNROLL)
        tail = m_s[128:136, :].astype(BF16)
        ab_s[128:136, :] = dot(tail, kv[64], ((1,), (1,)))
        ab_s[136:144, :] = jnp.zeros((8, ROW), F32)
        if first:
            load(2).wait()
        out = dot3(ti_ref, ab_s[...])
        low = out[0:32] - pltpu.roll(out[64:96], 64, 1)
        high = pltpu.roll(out[32:64], 64, 1) - out[96:128]
        return jnp.where(left_half, low, high)

    def adjoint(packed, dst):
        turned = pltpu.roll(packed, 64, 1)
        doubled = jnp.concatenate(
            [jnp.where(left_half, packed, turned), jnp.where(left_half, turned, packed)], axis=0
        )
        out = dot(ta_ref[...], stacked(doubled))
        l_s[...] = jnp.where(left_half, out[:ROWS], out[ROWS:])

        def step(i, carry):
            rows = l_s[pl.ds(pl.multiple_of(8 * i, 8), 8), :]
            moved = jnp.concatenate(
                [jnp.where(group_row == j, rows, 0.0) for j in range(4)], axis=1
            ).astype(BF16)
            weights = kv[pl.ds(4 * i, 4)].reshape(512, 256)
            q_s[pl.ds(pl.multiple_of(8 * i, 8), 8), :] = dot(moved, weights)
            return carry

        lax.fori_loop(0, 16, step, 0, unroll=UNROLL)
        q_s[128:136, :] = dot(l_s[128:136, :].astype(BF16), kv[64])
        q_s[136:144, :] = jnp.zeros((8, 256), F32)
        out = dot3(ts_ref, q_s[...])
        dst[0:8] = out[:, :ROW].reshape(8, 8, ROW)
        dst[8:16] = out[:, ROW:].reshape(8, 8, ROW)

    def sum_start(n, packed):
        send1[n] = packed
        ya[n, my] = packed[0:16]
        zb[n, mz] = packed[16:32]
        for who in y_ids:
            send(send1.at[n, pl.ds(0, 16)], ya.at[n, my], who, ar_ssem.at[n, 0], ar_rsem.at[n, 0])
        for who in z_ids:
            send(send1.at[n, pl.ds(16, 16)], zb.at[n, mz], who, ar_ssem.at[n, 1], ar_rsem.at[n, 1])

    def sum_middle(n):
        wait_for(zb.at[n, pl.ds(0, NZ - 1)], ar_rsem.at[n, 1])
        part = jnp.sum(zb[n], axis=0)
        mid_b[n] = part
        yb[n, my] = part
        for who in y_ids:
            send(mid_b.at[n], yb.at[n, my], who, ar_ssem.at[n, 2], ar_rsem.at[n, 2])
        wait_for(ya.at[n, pl.ds(0, NY - 1)], ar_rsem.at[n, 0])
        part = jnp.sum(ya[n], axis=0)
        mid_a[n] = part
        za[n, mz] = part
        for who in z_ids:
            send(mid_a.at[n], za.at[n, mz], who, ar_ssem.at[n, 3], ar_rsem.at[n, 3])

    def sum_end(n):
        wait_for(za.at[n, pl.ds(0, NZ - 1)], ar_rsem.at[n, 3])
        wait_for(yb.at[n, pl.ds(0, NY - 1)], ar_rsem.at[n, 2])
        return jnp.concatenate([jnp.sum(za[n], axis=0), jnp.sum(yb[n], axis=0)], axis=0)

    def scalars_start(n, one, two):
        sc_send[n, pl.ds(0, 1), :] = one
        sc_send[n, pl.ds(1, 1), :] = two
        sy[n, my, pl.ds(0, 1), :] = one
        sy[n, my, pl.ds(1, 1), :] = two
        for who in y_ids:
            send(sc_send.at[n], sy.at[n, my], who, sc_ssem.at[n, 0], sc_rsem.at[n, 0])

    def scalars_middle(n):
        wait_for(sy.at[n, pl.ds(0, NY - 1)], sc_rsem.at[n, 0])
        part = jnp.sum(sy[n], axis=0)
        sc_mid[n] = part
        sz[n, mz] = part
        for who in z_ids:
            send(sc_mid.at[n], sz.at[n, mz], who, sc_ssem.at[n, 1], sc_rsem.at[n, 1])

    def response_start(n, packed):
        row = jnp.sum(packed * packed, axis=0, keepdims=True)
        rs_send[n] = row
        rs_buf[n, ms] = row
        for p in s_nums:
            send(rs_send.at[n], rs_buf.at[n, ms], {"sensor": p}, rs_ssem.at[n], rs_rsem.at[n])

    def step_size(n):
        wait_for(sz.at[n, pl.ds(0, NZ - 1)], sc_rsem.at[n, 1])
        wait_for(rs_buf.at[n, pl.ds(0, NSEN - 1)], rs_rsem.at[n])
        sums = jnp.sum(sz[n], axis=0)
        total = jnp.sum(sums, axis=1, keepdims=True)
        response = jnp.sum(jnp.sum(rs_buf[n], axis=0), axis=1, keepdims=True)
        return total[0:1] / (response + total[1:2] + TINY)

    def scatter_start(n):
        rs_in[n, ms] = gp[n, ms]
        for p in s_nums:
            send(gp.at[n, p], rs_in.at[n, ms], {"sensor": p}, gr_ssem.at[n, 0], gr_rsem.at[n, 0])

    def scatter_end(n):
        wait_for(rs_in.at[n, pl.ds(0, NSEN - 1)], gr_rsem.at[n, 0])
        return jnp.sum(rs_in[n], axis=0)

    def gather(n, piece):
        b_s[1 + n] = piece
        g_s[n, ms] = piece
        for p in s_nums:
            send(b_s.at[1 + n], g_s.at[n, ms], {"sensor": p}, gr_ssem.at[n, 1], gr_rsem.at[n, 1])
        wait_for(g_s.at[n, pl.ds(0, NSEN - 1)], gr_rsem.at[n, 1])
        send(g_s.at[n, pl.ds(8, 8)], gh_n.at[n], nxt_id, gh_ssem.at[n, 0], gh_rsem.at[n, 0])
        send(g_s.at[n, pl.ds(0, 8)], gh_s.at[n], prv_id, gh_ssem.at[n, 1], gh_rsem.at[n, 1])
        return g_s[n, 0:8].reshape(NT, ROW), g_s[n, 8:16].reshape(NT, ROW)

    def halo(n):
        wait_for(gh_n.at[n], gh_rsem.at[n, 0])
        wait_for(gh_s.at[n], gh_rsem.at[n, 1])
        return gh_n[n].reshape(NT, ROW), gh_s[n].reshape(NT, ROW)

    def jumps(dst, above, first, second, below):
        rows = (first, second)
        for r in range(2):
            dst[r] = jnp.where(linked[0][r], pltpu.roll(rows[r], ROW - 1, 1) - rows[r], 0.0)
            dst[2 + r] = jnp.where(linked[1][r], pltpu.roll(rows[r], 1, 1) - rows[r], 0.0)
            north = above if r == 0 else first
            south = second if r == 0 else below
            dst[4 + r] = jnp.where(linked[2][r], north - rows[r], 0.0)
            dst[6 + r] = jnp.where(linked[3][r], south - rows[r], 0.0)

    def squares(refs):
        total = jnp.zeros((1, ROW), F32)
        for value in refs:
            total = total + jnp.sum(value * value, axis=0, keepdims=True)
        return total

    def divergence(v):
        for r in range(2):
            total = jnp.where(linked[1][r], pltpu.roll(v[r], 1, 1), 0.0)
            total = total + jnp.where(linked[0][r], pltpu.roll(v[2 + r], ROW - 1, 1), 0.0)
            if r == 0:
                total = total + jnp.where(linked[3][0], v[5], 0.0)
            else:
                total = total + jnp.where(linked[2][1], v[6], 0.0)
            for k in range(4):
                total = total - jnp.where(linked[k][r], v[2 * k + r], 0.0)
            dt_s[8 * r : 8 * r + 8] = total.reshape(8, 8, ROW)

    load(0).wait()
    load(1).wait()
    first_sum = forward(x0_ref[...], True)
    prepare()
    own = cell * (2 * ROW) + lax.broadcasted_iota(jnp.int32, (1, 2 * ROW), 1)
    linked = [[None, None] for _ in range(4)]
    edges = []
    for k in range(4):
        both = jnp.where(nb_ref[pl.ds(k, 1), :] != own, 1.0, 0.0)
        linked[k][0] = both[:, :ROW] > 0.5
        linked[k][1] = both[:, ROW:] > 0.5
        if k >= 2:
            edges.append(both[:, :ROW] if k == 2 else both[:, ROW:])
    edge_link = jnp.where(half == 0, edges[0], edges[1]) > 0.5
    load(6).wait()
    pl.semaphore_wait(barrier, len(everyone))
    sum_start(0, first_sum)
    sum_middle(0)
    lanes = pl.multiple_of(ROW * (1 - half), ROW)
    times = pl.multiple_of(8 * tb, 8)
    send(
        m0_ref.at[3 - half, pl.ds(times, 8), pl.ds(lanes, ROW)], h_m, edge_id,
        h_ssem.at[0], h_rsem.at[0],
    )
    send(thr_s.at[1 - half], h_t, edge_id, h_ssem.at[1], h_rsem.at[1])
    divergence([m0_ref[k, :, r * ROW : (r + 1) * ROW] for k in range(4) for r in range(2)])
    for i in (7, 8, 9):
        load(i).wait()
    observed = jnp.concatenate([obs_ref[0:32], obs_ref[32:64]], axis=1)
    misfit = sum_end(0) - observed

    adjoint(misfit, gp.at[0])
    scatter_start(0)
    send(x0_ref.at[:, pl.ds(ROW, ROW)], hx_n, nxt_id, h_ssem.at[2], h_rsem.at[2])
    send(x0_ref.at[:, pl.ds(0, ROW)], hx_s, prv_id, h_ssem.at[3], h_rsem.at[3])
    wait_for(h_m, h_rsem.at[0])
    wait_for(h_t, h_rsem.at[1])
    extra = dt_s[ms] + jnp.where(edge_link, h_m[...], 0.0)
    piece = scatter_end(0)
    b_s[0] = piece
    grad_a, grad_b = gather(0, piece + extra)
    part = forward(jnp.concatenate([grad_a, grad_b], axis=1), False)
    sum_start(1, part)
    above, below = halo(0)
    grad_a = g_s[0, 0:8].reshape(NT, ROW)
    grad_b = g_s[0, 8:16].reshape(NT, ROW)
    jumps(gj_s, above, grad_a, grad_b, below)
    scalars_start(0, squares([grad_a, grad_b]), squares([gj_s[i] for i in range(8)]))
    sum_middle(1)
    scalars_middle(0)
    response = sum_end(1)
    response_start(0, response)
    adjoint(response, gp.at[1])
    scatter_start(1)
    wait_for(hx_n, h_rsem.at[2])
    wait_for(hx_s, h_rsem.at[3])
    jumps(jump_s, hx_n[...], x0_ref[:, 0:ROW], x0_ref[:, ROW:], hx_s[...])
    size = step_size(0)
    penalty = []
    thresholds = [thr_s[0, 0:1], thr_s[1, 0:1]]
    for i in range(8):
        moved = jump_s[i] - size * gj_s[i]
        jump_s[i] = moved
        limit = thresholds[i % 2]
        shifted = moved + m0_ref[i // 2, :, (i % 2) * ROW : (i % 2 + 1) * ROW]
        shrunk = jnp.maximum(shifted - limit, 0.0) - jnp.maximum(-shifted - limit, 0.0)
        rest = shifted - shrunk
        mult_s[i] = rest
        penalty.append(moved - shrunk + rest)
    divergence(penalty)
    moved = -jump_s[4 + 3 * half, pl.ds(times, 8), :]
    shifted = moved + h_m[...]
    limit = h_t[...]
    shrunk = jnp.maximum(shifted - limit, 0.0) - jnp.maximum(-shifted - limit, 0.0)
    extra = dt_s[ms] + jnp.where(edge_link, moved - shrunk + (shifted - shrunk), 0.0)
    est_ref[:, 0:ROW] = x0_ref[:, 0:ROW] - size * g_s[0, 0:8].reshape(NT, ROW)
    est_ref[:, ROW:] = x0_ref[:, ROW:] - size * g_s[0, 8:16].reshape(NT, ROW)

    piece = b_s[0] - size * scatter_end(1)
    grad_a, grad_b = gather(1, piece + extra)
    part = forward(jnp.concatenate([grad_a, grad_b], axis=1), False)
    sum_start(2, part)
    above, below = halo(1)
    grad_a = g_s[1, 0:8].reshape(NT, ROW)
    grad_b = g_s[1, 8:16].reshape(NT, ROW)
    jumps(gj_s, above, grad_a, grad_b, below)
    scalars_start(1, squares([grad_a, grad_b]), squares([gj_s[i] for i in range(8)]))
    sum_middle(2)
    scalars_middle(1)
    response_start(1, sum_end(2))
    size = step_size(1)
    est_ref[:, 0:ROW] = est_ref[:, 0:ROW] - size * g_s[1, 0:8].reshape(NT, ROW)
    est_ref[:, ROW:] = est_ref[:, ROW:] - size * g_s[1, 8:16].reshape(NT, ROW)
    for i in range(8):
        shifted = jump_s[i] - size * gj_s[i] + mult_s[i]
        limit = thresholds[i % 2]
        shrunk = jnp.maximum(shifted - limit, 0.0) - jnp.maximum(-shifted - limit, 0.0)
        k, r = i // 2, i % 2
        aux_ref[k, :, r * ROW : (r + 1) * ROW] = shrunk
        mul_ref[k, :, r * ROW : (r + 1) * ROW] = shifted - shrunk

    for i, view in enumerate((h_m, h_t, hx_n, hx_s)):
        wait_for(view, h_ssem.at[i])
    for n in range(3):
        wait_for(ya.at[n, pl.ds(0, NY - 1)], ar_ssem.at[n, 0])
        wait_for(zb.at[n, pl.ds(0, NZ - 1)], ar_ssem.at[n, 1])
        wait_for(yb.at[n, pl.ds(0, NY - 1)], ar_ssem.at[n, 2])
        wait_for(za.at[n, pl.ds(0, NZ - 1)], ar_ssem.at[n, 3])
    for n in range(2):
        wait_for(sy.at[n, pl.ds(0, NY - 1)], sc_ssem.at[n, 0])
        wait_for(sz.at[n, pl.ds(0, NZ - 1)], sc_ssem.at[n, 1])
        wait_for(rs_buf.at[n, pl.ds(0, NSEN - 1)], rs_ssem.at[n])
        wait_for(rs_in.at[n, pl.ds(0, NSEN - 1)], gr_ssem.at[n, 0])
        wait_for(g_s.at[n, pl.ds(0, NSEN - 1)], gr_ssem.at[n, 1])
        wait_for(gh_n.at[n], gh_ssem.at[n, 0])
        wait_for(gh_s.at[n], gh_ssem.at[n, 1])


def finish(est, aux, mul, est_out, aux_out, mul_out, sems):
    copies = [
        pltpu.make_async_copy(src, dst, sems.at[i])
        for i, (src, dst) in enumerate(((aux, aux_out), (mul, mul_out), (est, est_out)))
    ]
    for copy in copies:
        copy.start()
    for copy in copies:
        copy.wait()


def per_device(kernel, observed, start_model, start_multiplier, neighbours, tile, weight):
    hbm = pl.BlockSpec(memory_space=pltpu.HBM)
    vmem = pl.BlockSpec(memory_space=pltpu.VMEM)
    scratch = lambda *shape, dtype=F32: pltpu.VMEM(shape, dtype)
    dma = lambda *shape: pltpu.SemaphoreType.DMA(shape)
    analysis, back, synthesis, closing = (jnp.asarray(t) for t in tables())
    inputs = (
        kernel, observed, start_model, start_multiplier, neighbours, tile.reshape(1, 256),
        weight.reshape(1, 64), analysis, back, synthesis, closing,
    )
    results = pl.pallas_call(
        body,
        out_shape=(
            jax.ShapeDtypeStruct((NT, 256), F32),
            jax.ShapeDtypeStruct((4, NT, 256), F32),
            jax.ShapeDtypeStruct((4, NT, 256), F32),
        ),
        in_specs=[hbm] * 11,
        out_specs=(vmem, vmem, vmem),
        scratch_shapes=[
            scratch(NF, 128, 256, dtype=BF16),
            scratch(NT, 64),
            scratch(NT, 256),
            scratch(4, NT, 256),
            scratch(4, 256, dtype=jnp.int32),
            scratch(1, 256, dtype=jnp.int32),
            scratch(1, 64),
            scratch(ROWS, 256, dtype=BF16),
            scratch(2 * ROWS, 256, dtype=BF16),
            scratch(2, 128, ROWS, dtype=BF16),
            scratch(2, NT, ROWS, dtype=BF16),
            scratch(ROWS, 256),
            scratch(ROWS, ROW),
            scratch(ROWS, ROW),
            scratch(ROWS, 256),
            scratch(3, 32, ROW),
            scratch(3, NY, 16, ROW),
            scratch(3, NZ, 16, ROW),
            scratch(3, NZ, 16, ROW),
            scratch(3, NY, 16, ROW),
            scratch(3, 16, ROW),
            scratch(3, 16, ROW),
            scratch(2, 2, ROW),
            scratch(2, 2, ROW),
            scratch(2, NY, 2, ROW),
            scratch(2, NZ, 2, ROW),
            scratch(2, 1, ROW),
            scratch(2, NSEN, 1, ROW),
            scratch(2, 16, 8, ROW),
            scratch(2, NSEN, 8, ROW),
            scratch(2, 16, 8, ROW),
            scratch(3, 8, ROW),
            scratch(16, 8, ROW),
            scratch(2, 8, ROW),
            scratch(8, ROW),
            scratch(8, ROW),
            scratch(NT, ROW),
            scratch(NT, ROW),
            scratch(2, 8, 8, ROW),
            scratch(2, 8, 8, ROW),
            scratch(8, NT, ROW),
            scratch(8, NT, ROW),
            scratch(8, NT, ROW),
            dma(2, 4),
            dma(10),
            dma(4),
            dma(4),
            dma(3, 4),
            dma(3, 4),
            dma(2, 2),
            dma(2, 2),
            dma(2),
            dma(2),
            dma(2, 2),
            dma(2, 2),
            dma(2, 2),
            dma(2, 2),
        ],
        compiler_params=pltpu.CompilerParams(
            collective_id=0, has_side_effects=True, vmem_limit_bytes=MAIN_VMEM
        ),
        name="inversion",
    )(*(pltpu.with_memory_space_constraint(x, pltpu.HBM) for x in inputs))
    return pl.pallas_call(
        finish,
        out_shape=tuple(jax.ShapeDtypeStruct(r.shape, F32) for r in results),
        in_specs=[vmem] * 3,
        out_specs=(hbm, hbm, hbm),
        scratch_shapes=[dma(3)],
        compiler_params=pltpu.CompilerParams(vmem_limit_bytes=1024 * 1024),
        name="finish",
    )(*results)


def solution(mesh):
    split_mesh = Mesh(mesh.devices.reshape(NY, NZ, NSEN), ("y", "zh", "sensor"))
    cells = ("y", "zh")
    in_specs = (
        P(None, None, "sensor", cells),
        P(None, "sensor"),
        P(None, cells),
        P(None, None, cells),
        P(None, cells),
        P(cells),
        P(),
    )
    out_specs = (P(None, cells), P(None, None, cells), P(None, None, cells))
    return jax.shard_map(
        per_device, mesh=split_mesh, in_specs=in_specs, out_specs=out_specs, check_vma=False
    )
```

```python
import functools

import jax
import jax.numpy as jnp
import numpy as np
from jax import lax
from jax.experimental import pallas as pl
from jax.experimental.pallas import tpu as pltpu
from jax.sharding import Mesh
from jax.sharding import PartitionSpec as P

NT = 64
NF = 65
ROW = 128
NY = 8
NZ = 4
NSEN = 16
ROWS = 144
SHRINK_SCALE = 0.4
TINY = 1e-06
MAIN_VMEM = 40 * 1024 * 1024
F32 = jnp.float32
BF16 = jnp.bfloat16
MESH = pl.DeviceIdType.MESH
Y_ORDER = (4, 3, 5, 2, 6, 1, 7)
Z_ORDER = (2, 1, 3)


def high_low(table):
    high = table.astype(BF16)
    low = (table - high.astype(np.float32)).astype(BF16)
    return high, low


def tables():
    freq = np.arange(NF)[:, None]
    time = np.arange(NT)[None, :]
    phase = 2.0 * np.pi * (freq * time % (2 * NT)) / (2 * NT)
    cosine, sine = np.cos(phase), np.sin(phase)
    weight = np.where((freq == 0) | (freq == NF - 1), 1.0, 2.0) / (2 * NT)
    wcos, wsin = cosine * weight, sine * weight

    def interleaved(even, odd):
        out = np.zeros((ROWS, NT), np.float32)
        out[0 : 2 * NF : 2] = even
        out[1 : 2 * NF : 2] = odd
        return out

    analysis = interleaved(cosine, -sine)
    back = np.concatenate([interleaved(wcos, -wsin), interleaved(-wsin, -wcos)], axis=0)
    synthesis = np.concatenate([interleaved(wcos, -wsin).T, interleaved(wsin, wcos).T], axis=0)
    ah, al = high_low(analysis)
    bh, bl = high_low(back)
    sh, sl = high_low(synthesis)
    ch, cl = high_low(analysis.T)
    return (
        np.concatenate([ah, al, ah, al], axis=1),
        np.concatenate([bh, bl, bh, bl], axis=1),
        np.stack([sh, sl]),
        np.stack([ch, cl]),
    )


def split(value):
    high = value.astype(BF16)
    return high, (value - high.astype(F32)).astype(BF16)


def dot(left, right, dims=((1,), (0,))):
    return lax.dot_general(left, right, (dims, ((), ())), preferred_element_type=F32)


def dot3(table_ref, value):
    high, low = split(value)
    th = table_ref[0]
    return dot(th, high) + dot(th, low) + dot(table_ref[1], high)


def stacked(value):
    high, low = split(value)
    return jnp.concatenate([high, high, low, low], axis=0)


def body(
    k_hbm, obs_hbm, x0_hbm, m0_hbm, nb_hbm, tile_hbm, w_hbm, tf_hbm, ta_hbm, ti_hbm, ts_hbm,
    est_ref, aux_ref, mul_ref,
    kv, obs_ref, x0_ref, m0_ref, nb_ref, tile_ref, w_ref, tf_ref, ta_ref, ti_ref, ts_ref, m_s, ab_s, l_s, q_s,
    send1, ya, zb, za, yb, mid_a, mid_b,
    sc_send, sc_mid, sy, sz, rs_send, rs_buf,
    gp, rs_in, g_s, b_s, dt_s, thr_s, h_m, h_t, hx_n, hx_s, gh_n, gh_s,
    jump_s, gj_s, mult_s,
    k_sem, in_sem, h_ssem, h_rsem, ar_ssem, ar_rsem, sc_ssem, sc_rsem, rs_ssem, rs_rsem, gr_ssem, gr_rsem,
    gh_ssem, gh_rsem,
):
    my = lax.axis_index("y")
    mz = lax.axis_index("zh")
    ms = lax.axis_index("sensor")
    cell = my * NZ + mz
    nxt = (cell + 1) % (NY * NZ)
    prv = (cell + NY * NZ - 1) % (NY * NZ)
    nxt_id = {"y": nxt // NZ, "zh": nxt % NZ}
    prv_id = {"y": prv // NZ, "zh": prv % NZ}
    y_ids = [{"y": (my + j) % NY} for j in Y_ORDER]
    z_ids = [{"zh": (mz + j) % NZ} for j in Z_ORDER]
    s_nums = [(ms + j) % NSEN for j in (7, 9, 6, 10, 5, 11, 4, 12, 3, 13, 8, 2, 14, 1, 15)]

    tb = ms % 8
    half = ms // 8
    edge = (cell + NY * NZ + 1 - 2 * half) % (NY * NZ)
    edge_id = {"y": edge // NZ, "zh": edge % NZ}

    def load(i):
        src, dst = loads[i]
        return pltpu.make_async_copy(src, dst, in_sem.at[i])

    loads = (
        (x0_hbm, x0_ref), (tf_hbm, tf_ref), (ti_hbm, ti_ref), (w_hbm, w_ref), (tile_hbm, tile_ref),
        (nb_hbm, nb_ref), (m0_hbm, m0_ref), (obs_hbm, obs_ref), (ta_hbm, ta_ref), (ts_hbm, ts_ref),
    )
    load(0).start()
    load(1).start()

    bounds = (0, 16, 32, 48, 56, 65)

    def k_copy(plane, q):
        lo, hi = bounds[q], bounds[q + 1]
        return pltpu.make_async_copy(
            k_hbm.at[plane, pl.ds(lo, hi - lo)],
            kv.at[pl.ds(lo, hi - lo), pl.ds(64 * plane, 64)],
            k_sem.at[plane, q],
        )

    for q in range(len(bounds) - 1):
        for plane in range(2):
            k_copy(plane, q).start()
    barrier = pltpu.get_barrier_semaphore()
    everyone = y_ids + z_ids + [{"sensor": p} for p in s_nums] + [nxt_id, prv_id]
    for who in everyone:
        pl.semaphore_signal(barrier, inc=1, device_id=who, device_id_type=MESH)

    for i in range(2, 10):
        load(i).start()

    def send(src, dst, who, ssem, rsem):
        pltpu.make_async_remote_copy(
            src_ref=src, dst_ref=dst, send_sem=ssem, recv_sem=rsem, device_id=who,
            device_id_type=MESH,
        ).start()

    def wait_for(view, sem):
        pltpu.make_async_copy(view, view, sem).wait()

    lane = lax.broadcasted_iota(jnp.int32, (1, ROW), 1)
    left_half = lane < 64

    def prepare():
        for i in (3, 4, 5):
            load(i).wait()
        column = jnp.sum(
            jnp.where(
                lax.broadcasted_iota(jnp.int32, (64, 64), 0)
                == lax.broadcasted_iota(jnp.int32, (64, 64), 1),
                jnp.broadcast_to(w_ref[...], (64, 64)), 0.0,
            ),
            axis=1, keepdims=True,
        )
        labels = lax.broadcasted_iota(jnp.int32, (64, 2 * ROW), 0)
        threshold = SHRINK_SCALE * jnp.sum(
            jnp.where(labels == tile_ref[...], column, 0.0), axis=0, keepdims=True
        )
        thr_s[0] = jnp.broadcast_to(threshold[:, :ROW], (8, ROW))
        thr_s[1] = jnp.broadcast_to(threshold[:, ROW:], (8, ROW))

    group_row = lax.broadcasted_iota(jnp.int32, (8, ROW), 0) // 2

    def block_rows(i):
        return pl.ds(pl.multiple_of(8 * i, 8), 8)

    def own_rows(out):
        kept = out[:, 0:ROW]
        for j in range(1, 4):
            kept = jnp.where(group_row == j, out[:, j * ROW : (j + 1) * ROW], kept)
        return kept

    def cells(h):
        return pl.ds(pl.multiple_of(ROW * h, ROW), ROW)

    def forward_start(field):
        for h in range(2):
            m_s[h] = dot(tf_ref[...], stacked(field[:, h * ROW : (h + 1) * ROW]))

        def step(i, carry):
            moved = jnp.concatenate([m_s[0, block_rows(i), :], m_s[1, block_rows(i), :]], axis=1)
            weights = kv[pl.ds(4 * i, 4)].reshape(512, 256)
            ab_s[block_rows(i), :] = own_rows(dot(moved.astype(BF16), weights, ((1,), (1,))))
            return carry

        for q in range(len(bounds) - 1):
            k_copy(0, q).wait()
            k_copy(1, q).wait()
            lo, hi = bounds[q] // 4, min(bounds[q + 1] // 4, 16)
            lax.fori_loop(lo, hi, step, 0, unroll=hi - lo)
        tail = jnp.concatenate([m_s[0, 128:136, :], m_s[1, 128:136, :]], axis=1).astype(BF16)
        ab_s[128:136, :] = dot(tail, kv[64], ((1,), (1,)))
        ab_s[136:144, :] = jnp.zeros((8, ROW), F32)

    def forward_half(field, h, adds):
        m_s[h] = dot(tf_ref[...], stacked(field))

        def step(i, carry):
            moved = m_s[h, block_rows(i), :].astype(BF16)
            weights = kv[pl.ds(4 * i, 4), :, cells(h)].reshape(512, ROW)
            kept = own_rows(dot(moved, weights, ((1,), (1,))))
            ab_s[block_rows(i), :] = ab_s[block_rows(i), :] + kept if adds else kept
            return carry

        lax.fori_loop(0, 16, step, 0, unroll=16)
        tail = dot(m_s[h, 128:136, :].astype(BF16), kv[64, :, cells(h)], ((1,), (1,)))
        ab_s[128:136, :] = ab_s[128:136, :] + tail if adds else tail

    def forward_end():
        out = dot3(ti_ref, ab_s[...])
        low = out[0:32] - pltpu.roll(out[64:96], 64, 1)
        high = pltpu.roll(out[32:64], 64, 1) - out[96:128]
        return jnp.where(left_half, low, high)

    def adjoint(packed, n):
        turned = pltpu.roll(packed, 64, 1)
        doubled = jnp.concatenate(
            [jnp.where(left_half, packed, turned), jnp.where(left_half, turned, packed)], axis=0
        )
        out = dot(ta_ref[...], stacked(doubled))
        l_s[...] = jnp.where(left_half, out[:ROWS], out[ROWS:])

        for h, order in ((1 - half, (4, 3, 5, 2, 6, 1, 7, 0)), (half, (4, 3, 5, 2, 6, 1, 7))):

            def step(i, carry):
                rows = l_s[block_rows(i), :]
                moved = jnp.concatenate(
                    [jnp.where(group_row == j, rows, 0.0) for j in range(4)], axis=1
                ).astype(BF16)
                weights = kv[pl.ds(4 * i, 4), :, cells(h)].reshape(512, ROW)
                q_s[h, block_rows(i), :] = dot(moved, weights)
                return carry

            lax.fori_loop(0, 16, step, 0, unroll=16)
            q_s[h, 128:136, :] = dot(l_s[128:136, :].astype(BF16), kv[64, :, cells(h)])
            q_s[h, 136:144, :] = jnp.zeros((8, ROW), F32)
            out = dot3(ts_ref, q_s[h])
            gp[n, pl.ds(8 * h, 8)] = out.reshape(8, 8, ROW)
            for j in order:
                p = 8 * h + (tb + j) % 8
                send(gp.at[n, p], rs_in.at[n, ms], {"sensor": p}, gr_ssem.at[n, 0], gr_rsem.at[n, 0])
        rs_in[n, ms] = gp[n, ms]

    def sum_start(n, packed):
        send1[n] = packed
        ya[n, my] = packed[0:16]
        zb[n, mz] = packed[16:32]
        for who in y_ids:
            send(send1.at[n, pl.ds(0, 16)], ya.at[n, my], who, ar_ssem.at[n, 0], ar_rsem.at[n, 0])
        for who in z_ids:
            send(send1.at[n, pl.ds(16, 16)], zb.at[n, mz], who, ar_ssem.at[n, 1], ar_rsem.at[n, 1])

    def sum_middle(n):
        wait_for(zb.at[n, pl.ds(0, NZ - 1)], ar_rsem.at[n, 1])
        part = jnp.sum(zb[n], axis=0)
        mid_b[n] = part
        yb[n, my] = part
        for who in y_ids:
            send(mid_b.at[n], yb.at[n, my], who, ar_ssem.at[n, 2], ar_rsem.at[n, 2])
        wait_for(ya.at[n, pl.ds(0, NY - 1)], ar_rsem.at[n, 0])
        part = jnp.sum(ya[n], axis=0)
        mid_a[n] = part
        za[n, mz] = part
        for who in z_ids:
            send(mid_a.at[n], za.at[n, mz], who, ar_ssem.at[n, 3], ar_rsem.at[n, 3])

    def sum_end(n):
        wait_for(za.at[n, pl.ds(0, NZ - 1)], ar_rsem.at[n, 3])
        wait_for(yb.at[n, pl.ds(0, NY - 1)], ar_rsem.at[n, 2])
        return jnp.concatenate([jnp.sum(za[n], axis=0), jnp.sum(yb[n], axis=0)], axis=0)

    def scalars_start(n, one, two):
        sc_send[n, pl.ds(0, 1), :] = one
        sc_send[n, pl.ds(1, 1), :] = two
        sy[n, my, pl.ds(0, 1), :] = one
        sy[n, my, pl.ds(1, 1), :] = two
        for who in y_ids:
            send(sc_send.at[n], sy.at[n, my], who, sc_ssem.at[n, 0], sc_rsem.at[n, 0])

    def scalars_middle(n):
        wait_for(sy.at[n, pl.ds(0, NY - 1)], sc_rsem.at[n, 0])
        part = jnp.sum(sy[n], axis=0)
        sc_mid[n] = part
        sz[n, mz] = part
        for who in z_ids:
            send(sc_mid.at[n], sz.at[n, mz], who, sc_ssem.at[n, 1], sc_rsem.at[n, 1])

    def response_start(n, packed):
        row = jnp.sum(packed * packed, axis=0, keepdims=True)
        rs_send[n] = row
        rs_buf[n, ms] = row
        for p in s_nums:
            send(rs_send.at[n], rs_buf.at[n, ms], {"sensor": p}, rs_ssem.at[n], rs_rsem.at[n])

    def step_size(n):
        wait_for(sz.at[n, pl.ds(0, NZ - 1)], sc_rsem.at[n, 1])
        wait_for(rs_buf.at[n, pl.ds(0, NSEN - 1)], rs_rsem.at[n])
        sums = jnp.sum(sz[n], axis=0)
        total = jnp.sum(sums, axis=1, keepdims=True)
        response = jnp.sum(jnp.sum(rs_buf[n], axis=0), axis=1, keepdims=True)
        return total[0:1] / (response + total[1:2] + TINY)

    def scatter_end(n):
        wait_for(rs_in.at[n, pl.ds(0, NSEN - 1)], gr_rsem.at[n, 0])
        return jnp.sum(rs_in[n], axis=0)

    def gather_forward(n, piece):
        b_s[1 + n] = piece
        g_s[n, ms] = piece
        src, dst = b_s.at[1 + n], g_s.at[n, ms]
        for j in (4, 3, 5, 2, 6, 1, 7, 0):
            who = {"sensor": 8 * (1 - half) + (tb + j) % 8}
            send(src, dst, who, gr_ssem.at[n, 1], gr_rsem.at[n, 1])
        for j in (4, 3, 5, 2, 6, 1, 7):
            who = {"sensor": 8 * half + (tb + j) % 8}
            send(src, dst, who, gr_ssem.at[n, 2], gr_rsem.at[n, 2])
        wait_for(g_s.at[n, pl.ds(0, 7)], gr_rsem.at[n, 2])
        forward_half(g_s[n, pl.ds(8 * half, 8)].reshape(NT, ROW), half, False)
        wait_for(g_s.at[n, pl.ds(0, 8)], gr_rsem.at[n, 1])
        send(g_s.at[n, pl.ds(8, 8)], gh_n.at[n], nxt_id, gh_ssem.at[n, 0], gh_rsem.at[n, 0])
        send(g_s.at[n, pl.ds(0, 8)], gh_s.at[n], prv_id, gh_ssem.at[n, 1], gh_rsem.at[n, 1])
        forward_half(g_s[n, pl.ds(8 * (1 - half), 8)].reshape(NT, ROW), 1 - half, True)
        return forward_end()

    def halo(n):
        wait_for(gh_n.at[n], gh_rsem.at[n, 0])
        wait_for(gh_s.at[n], gh_rsem.at[n, 1])
        return gh_n[n].reshape(NT, ROW), gh_s[n].reshape(NT, ROW)

    def jumps(dst, above, first, second, below):
        rows = (first, second)
        for r in range(2):
            dst[r] = jnp.where(linked[0][r], pltpu.roll(rows[r], ROW - 1, 1) - rows[r], 0.0)
            dst[2 + r] = jnp.where(linked[1][r], pltpu.roll(rows[r], 1, 1) - rows[r], 0.0)
            north = above if r == 0 else first
            south = second if r == 0 else below
            dst[4 + r] = jnp.where(linked[2][r], north - rows[r], 0.0)
            dst[6 + r] = jnp.where(linked[3][r], south - rows[r], 0.0)

    def squares(refs):
        total = jnp.zeros((1, ROW), F32)
        for value in refs:
            total = total + jnp.sum(value * value, axis=0, keepdims=True)
        return total

    def divergence(v):
        for r in range(2):
            total = jnp.where(linked[1][r], pltpu.roll(v[r], 1, 1), 0.0)
            total = total + jnp.where(linked[0][r], pltpu.roll(v[2 + r], ROW - 1, 1), 0.0)
            if r == 0:
                total = total + jnp.where(linked[3][0], v[5], 0.0)
            else:
                total = total + jnp.where(linked[2][1], v[6], 0.0)
            for k in range(4):
                total = total - jnp.where(linked[k][r], v[2 * k + r], 0.0)
            dt_s[8 * r : 8 * r + 8] = total.reshape(8, 8, ROW)

    load(0).wait()
    load(1).wait()
    forward_start(x0_ref[...])
    load(2).wait()
    first_sum = forward_end()
    pl.semaphore_wait(barrier, len(everyone))
    sum_start(0, first_sum)
    prepare()
    own = cell * (2 * ROW) + lax.broadcasted_iota(jnp.int32, (1, 2 * ROW), 1)
    linked = [[None, None] for _ in range(4)]
    edges = []
    for k in range(4):
        both = jnp.where(nb_ref[pl.ds(k, 1), :] != own, 1.0, 0.0)
        linked[k][0] = both[:, :ROW] > 0.5
        linked[k][1] = both[:, ROW:] > 0.5
        if k >= 2:
            edges.append(both[:, :ROW] if k == 2 else both[:, ROW:])
    edge_link = jnp.where(half == 0, edges[0], edges[1]) > 0.5
    load(6).wait()
    sum_middle(0)
    lanes = pl.multiple_of(ROW * (1 - half), ROW)
    times = pl.multiple_of(8 * tb, 8)
    send(
        m0_ref.at[3 - half, pl.ds(times, 8), pl.ds(lanes, ROW)], h_m, edge_id,
        h_ssem.at[0], h_rsem.at[0],
    )
    send(thr_s.at[1 - half], h_t, edge_id, h_ssem.at[1], h_rsem.at[1])
    divergence([m0_ref[k, :, r * ROW : (r + 1) * ROW] for k in range(4) for r in range(2)])
    for i in (7, 8, 9):
        load(i).wait()
    observed = jnp.concatenate([obs_ref[0:32], obs_ref[32:64]], axis=1)
    misfit = sum_end(0) - observed

    adjoint(misfit, 0)
    send(x0_ref.at[:, pl.ds(ROW, ROW)], hx_n, nxt_id, h_ssem.at[2], h_rsem.at[2])
    send(x0_ref.at[:, pl.ds(0, ROW)], hx_s, prv_id, h_ssem.at[3], h_rsem.at[3])
    wait_for(h_m, h_rsem.at[0])
    wait_for(h_t, h_rsem.at[1])
    extra = dt_s[ms] + jnp.where(edge_link, h_m[...], 0.0)
    piece = scatter_end(0)
    b_s[0] = piece
    sum_start(1, gather_forward(0, piece + extra))
    above, below = halo(0)
    grad_a = g_s[0, 0:8].reshape(NT, ROW)
    grad_b = g_s[0, 8:16].reshape(NT, ROW)
    jumps(gj_s, above, grad_a, grad_b, below)
    scalars_start(0, squares([grad_a, grad_b]), squares([gj_s[i] for i in range(8)]))
    sum_middle(1)
    scalars_middle(0)
    response = sum_end(1)
    response_start(0, response)
    adjoint(response, 1)
    wait_for(hx_n, h_rsem.at[2])
    wait_for(hx_s, h_rsem.at[3])
    jumps(jump_s, hx_n[...], x0_ref[:, 0:ROW], x0_ref[:, ROW:], hx_s[...])
    size = step_size(0)
    penalty = []
    thresholds = [thr_s[0, 0:1], thr_s[1, 0:1]]
    for i in range(8):
        moved = jump_s[i] - size * gj_s[i]
        jump_s[i] = moved
        limit = thresholds[i % 2]
        shifted = moved + m0_ref[i // 2, :, (i % 2) * ROW : (i % 2 + 1) * ROW]
        shrunk = jnp.maximum(shifted - limit, 0.0) - jnp.maximum(-shifted - limit, 0.0)
        rest = shifted - shrunk
        mult_s[i] = rest
        penalty.append(moved - shrunk + rest)
    divergence(penalty)
    moved = -jump_s[4 + 3 * half, pl.ds(times, 8), :]
    shifted = moved + h_m[...]
    limit = h_t[...]
    shrunk = jnp.maximum(shifted - limit, 0.0) - jnp.maximum(-shifted - limit, 0.0)
    extra = dt_s[ms] + jnp.where(edge_link, moved - shrunk + (shifted - shrunk), 0.0)
    est_ref[:, 0:ROW] = x0_ref[:, 0:ROW] - size * g_s[0, 0:8].reshape(NT, ROW)
    est_ref[:, ROW:] = x0_ref[:, ROW:] - size * g_s[0, 8:16].reshape(NT, ROW)

    piece = b_s[0] - size * scatter_end(1)
    sum_start(2, gather_forward(1, piece + extra))
    above, below = halo(1)
    grad_a = g_s[1, 0:8].reshape(NT, ROW)
    grad_b = g_s[1, 8:16].reshape(NT, ROW)
    jumps(gj_s, above, grad_a, grad_b, below)
    scalars_start(1, squares([grad_a, grad_b]), squares([gj_s[i] for i in range(8)]))
    sum_middle(2)
    scalars_middle(1)
    response_start(1, sum_end(2))
    size = step_size(1)
    est_ref[:, 0:ROW] = est_ref[:, 0:ROW] - size * g_s[1, 0:8].reshape(NT, ROW)
    est_ref[:, ROW:] = est_ref[:, ROW:] - size * g_s[1, 8:16].reshape(NT, ROW)
    for i in range(8):
        shifted = jump_s[i] - size * gj_s[i] + mult_s[i]
        limit = thresholds[i % 2]
        shrunk = jnp.maximum(shifted - limit, 0.0) - jnp.maximum(-shifted - limit, 0.0)
        k, r = i // 2, i % 2
        aux_ref[k, :, r * ROW : (r + 1) * ROW] = shrunk
        mul_ref[k, :, r * ROW : (r + 1) * ROW] = shifted - shrunk

    for i, view in enumerate((h_m, h_t, hx_n, hx_s)):
        wait_for(view, h_ssem.at[i])
    for n in range(3):
        wait_for(ya.at[n, pl.ds(0, NY - 1)], ar_ssem.at[n, 0])
        wait_for(zb.at[n, pl.ds(0, NZ - 1)], ar_ssem.at[n, 1])
        wait_for(yb.at[n, pl.ds(0, NY - 1)], ar_ssem.at[n, 2])
        wait_for(za.at[n, pl.ds(0, NZ - 1)], ar_ssem.at[n, 3])
    for n in range(2):
        wait_for(sy.at[n, pl.ds(0, NY - 1)], sc_ssem.at[n, 0])
        wait_for(sz.at[n, pl.ds(0, NZ - 1)], sc_ssem.at[n, 1])
        wait_for(rs_buf.at[n, pl.ds(0, NSEN - 1)], rs_ssem.at[n])
        wait_for(rs_in.at[n, pl.ds(0, NSEN - 1)], gr_ssem.at[n, 0])
        wait_for(g_s.at[n, pl.ds(0, 8)], gr_ssem.at[n, 1])
        wait_for(g_s.at[n, pl.ds(0, 7)], gr_ssem.at[n, 2])
        wait_for(gh_n.at[n], gh_ssem.at[n, 0])
        wait_for(gh_s.at[n], gh_ssem.at[n, 1])


def finish(est, aux, mul, est_out, aux_out, mul_out, sems):
    copies = [
        pltpu.make_async_copy(src, dst, sems.at[i])
        for i, (src, dst) in enumerate(((aux, aux_out), (mul, mul_out), (est, est_out)))
    ]
    for copy in copies:
        copy.start()
    for copy in copies:
        copy.wait()


def per_device(kernel, observed, start_model, start_multiplier, neighbours, tile, weight):
    hbm = pl.BlockSpec(memory_space=pltpu.HBM)
    vmem = pl.BlockSpec(memory_space=pltpu.VMEM)
    scratch = lambda *shape, dtype=F32: pltpu.VMEM(shape, dtype)
    dma = lambda *shape: pltpu.SemaphoreType.DMA(shape)
    analysis, back, synthesis, closing = (jnp.asarray(t) for t in tables())
    inputs = (
        kernel, observed, start_model, start_multiplier, neighbours, tile.reshape(1, 256),
        weight.reshape(1, 64), analysis, back, synthesis, closing,
    )
    results = pl.pallas_call(
        body,
        out_shape=(
            jax.ShapeDtypeStruct((NT, 256), F32),
            jax.ShapeDtypeStruct((4, NT, 256), F32),
            jax.ShapeDtypeStruct((4, NT, 256), F32),
        ),
        in_specs=[hbm] * 11,
        out_specs=(vmem, vmem, vmem),
        scratch_shapes=[
            scratch(NF, 128, 256, dtype=BF16),
            scratch(NT, 64),
            scratch(NT, 256),
            scratch(4, NT, 256),
            scratch(4, 256, dtype=jnp.int32),
            scratch(1, 256, dtype=jnp.int32),
            scratch(1, 64),
            scratch(ROWS, 256, dtype=BF16),
            scratch(2 * ROWS, 256, dtype=BF16),
            scratch(2, 128, ROWS, dtype=BF16),
            scratch(2, NT, ROWS, dtype=BF16),
            scratch(2, ROWS, ROW),
            scratch(ROWS, ROW),
            scratch(ROWS, ROW),
            scratch(2, ROWS, ROW),
            scratch(3, 32, ROW),
            scratch(3, NY, 16, ROW),
            scratch(3, NZ, 16, ROW),
            scratch(3, NZ, 16, ROW),
            scratch(3, NY, 16, ROW),
            scratch(3, 16, ROW),
            scratch(3, 16, ROW),
            scratch(2, 2, ROW),
            scratch(2, 2, ROW),
            scratch(2, NY, 2, ROW),
            scratch(2, NZ, 2, ROW),
            scratch(2, 1, ROW),
            scratch(2, NSEN, 1, ROW),
            scratch(2, 16, 8, ROW),
            scratch(2, NSEN, 8, ROW),
            scratch(2, 16, 8, ROW),
            scratch(3, 8, ROW),
            scratch(16, 8, ROW),
            scratch(2, 8, ROW),
            scratch(8, ROW),
            scratch(8, ROW),
            scratch(NT, ROW),
            scratch(NT, ROW),
            scratch(2, 8, 8, ROW),
            scratch(2, 8, 8, ROW),
            scratch(8, NT, ROW),
            scratch(8, NT, ROW),
            scratch(8, NT, ROW),
            dma(2, 5),
            dma(10),
            dma(4),
            dma(4),
            dma(3, 4),
            dma(3, 4),
            dma(2, 2),
            dma(2, 2),
            dma(2),
            dma(2),
            dma(2, 3),
            dma(2, 3),
            dma(2, 2),
            dma(2, 2),
        ],
        compiler_params=pltpu.CompilerParams(
            collective_id=0, has_side_effects=True, vmem_limit_bytes=MAIN_VMEM
        ),
        name="inversion",
    )(*(pltpu.with_memory_space_constraint(x, pltpu.HBM) for x in inputs))
    return pl.pallas_call(
        finish,
        out_shape=tuple(jax.ShapeDtypeStruct(r.shape, F32) for r in results),
        in_specs=[vmem] * 3,
        out_specs=(hbm, hbm, hbm),
        scratch_shapes=[dma(3)],
        compiler_params=pltpu.CompilerParams(vmem_limit_bytes=1024 * 1024),
        name="finish",
    )(*results)


def solution(mesh):
    split_mesh = Mesh(mesh.devices.reshape(NY, NZ, NSEN), ("y", "zh", "sensor"))
    cells = ("y", "zh")
    in_specs = (
        P(None, None, "sensor", cells),
        P(None, "sensor"),
        P(None, cells),
        P(None, None, cells),
        P(None, cells),
        P(cells),
        P(),
    )
    out_specs = (P(None, cells), P(None, None, cells), P(None, None, cells))
    return jax.shard_map(
        per_device, mesh=split_mesh, in_specs=in_specs, out_specs=out_specs, check_vma=False
    )
```

```python
import functools

import jax
import jax.numpy as jnp
import numpy as np
from jax import lax
from jax.experimental import pallas as pl
from jax.experimental.pallas import tpu as pltpu
from jax.sharding import Mesh
from jax.sharding import PartitionSpec as P

NT = 64
NF = 65
ROW = 128
NY = 8
NZ = 4
NSEN = 16
ROWS = 144
SHRINK_SCALE = 0.4
TINY = 1e-06
MAIN_VMEM = 40 * 1024 * 1024
F32 = jnp.float32
BF16 = jnp.bfloat16
MESH = pl.DeviceIdType.MESH
Y_ORDER = (4, 3, 5, 2, 6, 1, 7)
Z_ORDER = (2, 1, 3)


def high_low(table):
    high = table.astype(BF16)
    low = (table - high.astype(np.float32)).astype(BF16)
    return high, low


def tables():
    freq = np.arange(NF)[:, None]
    time = np.arange(NT)[None, :]
    phase = 2.0 * np.pi * (freq * time % (2 * NT)) / (2 * NT)
    cosine, sine = np.cos(phase), np.sin(phase)
    weight = np.where((freq == 0) | (freq == NF - 1), 1.0, 2.0) / (2 * NT)
    wcos, wsin = cosine * weight, sine * weight

    def interleaved(even, odd):
        out = np.zeros((ROWS, NT), np.float32)
        out[0 : 2 * NF : 2] = even
        out[1 : 2 * NF : 2] = odd
        return out

    analysis = interleaved(cosine, -sine)
    back = np.concatenate([interleaved(wcos, -wsin), interleaved(-wsin, -wcos)], axis=0)
    synthesis = np.concatenate([interleaved(wcos, -wsin).T, interleaved(wsin, wcos).T], axis=0)
    ah, al = high_low(analysis)
    bh, bl = high_low(back)
    sh, sl = high_low(synthesis)
    ch, cl = high_low(analysis.T)
    return (
        np.concatenate([ah, al, ah, al], axis=1),
        np.concatenate([bh, bl, bh, bl], axis=1),
        np.stack([sh, sl]),
        np.stack([ch, cl]),
    )


def split(value):
    high = value.astype(BF16)
    return high, (value - high.astype(F32)).astype(BF16)


def dot(left, right, dims=((1,), (0,))):
    return lax.dot_general(left, right, (dims, ((), ())), preferred_element_type=F32)


def dot3(table_ref, value):
    high, low = split(value)
    th = table_ref[0]
    return dot(th, high) + dot(th, low) + dot(table_ref[1], high)


def stacked(value):
    high, low = split(value)
    return jnp.concatenate([high, high, low, low], axis=0)


def body(
    k_hbm, obs_hbm, x0_hbm, m0_hbm, nb_hbm, tile_hbm, w_hbm, tf_hbm, ta_hbm, ti_hbm, ts_hbm,
    est_ref, aux_ref, mul_ref,
    kv, obs_ref, x0_ref, m0_ref, nb_ref, tile_ref, w_ref, tf_ref, ta_ref, ti_ref, ts_ref, m_s, ab_s, l_s, q_s,
    send1, ya, zb, za, yb, mid_a, mid_b,
    sc_send, sc_mid, sy, sz, rs_send, rs_buf,
    gp, rs_in, g_s, b_s, dt_s, thr_s, h_m, h_t, hx_n, hx_s, gh_n, gh_s,
    jump_s, gj_s, mult_s,
    k_sem, in_sem, h_ssem, h_rsem, ar_ssem, ar_rsem, sc_ssem, sc_rsem, rs_ssem, rs_rsem, gr_ssem, gr_rsem,
    gh_ssem, gh_rsem,
):
    my = lax.axis_index("y")
    mz = lax.axis_index("zh")
    ms = lax.axis_index("sensor")
    cell = my * NZ + mz
    nxt = (cell + 1) % (NY * NZ)
    prv = (cell + NY * NZ - 1) % (NY * NZ)
    nxt_id = {"y": nxt // NZ, "zh": nxt % NZ}
    prv_id = {"y": prv // NZ, "zh": prv % NZ}
    y_ids = [{"y": (my + j) % NY} for j in Y_ORDER]
    z_ids = [{"zh": (mz + j) % NZ} for j in Z_ORDER]
    s_nums = [(ms + j) % NSEN for j in (7, 9, 6, 10, 5, 11, 4, 12, 3, 13, 8, 2, 14, 1, 15)]

    tb = ms % 8
    half = ms // 8
    edge = (cell + NY * NZ + 1 - 2 * half) % (NY * NZ)
    edge_id = {"y": edge // NZ, "zh": edge % NZ}

    def load(i):
        src, dst = loads[i]
        return pltpu.make_async_copy(src, dst, in_sem.at[i])

    loads = (
        (x0_hbm, x0_ref), (tf_hbm, tf_ref), (ti_hbm, ti_ref), (w_hbm, w_ref), (tile_hbm, tile_ref),
        (nb_hbm, nb_ref), (m0_hbm, m0_ref), (obs_hbm, obs_ref), (ta_hbm, ta_ref), (ts_hbm, ts_ref),
    )
    load(0).start()
    load(1).start()

    bounds = (0, 16, 32, 48, 56, 65)

    def k_copy(plane, q):
        lo, hi = bounds[q], bounds[q + 1]
        return pltpu.make_async_copy(
            k_hbm.at[plane, pl.ds(lo, hi - lo)],
            kv.at[pl.ds(lo, hi - lo), pl.ds(64 * plane, 64)],
            k_sem.at[plane, q],
        )

    barrier = pltpu.get_barrier_semaphore()
    everyone = y_ids + z_ids + [{"sensor": p} for p in s_nums] + [nxt_id, prv_id]
    for who in everyone:
        pl.semaphore_signal(barrier, inc=1, device_id=who, device_id_type=MESH)

    for q in range(len(bounds) - 1):
        for plane in range(2):
            k_copy(plane, q).start()
    for i in range(2, 10):
        load(i).start()

    def send(src, dst, who, ssem, rsem):
        pltpu.make_async_remote_copy(
            src_ref=src, dst_ref=dst, send_sem=ssem, recv_sem=rsem, device_id=who,
            device_id_type=MESH,
        ).start()

    def wait_for(view, sem):
        pltpu.make_async_copy(view, view, sem).wait()

    lane = lax.broadcasted_iota(jnp.int32, (1, ROW), 1)
    left_half = lane < 64

    def prepare():
        for i in (3, 4, 5):
            load(i).wait()
        column = jnp.sum(
            jnp.where(
                lax.broadcasted_iota(jnp.int32, (64, 64), 0)
                == lax.broadcasted_iota(jnp.int32, (64, 64), 1),
                jnp.broadcast_to(w_ref[...], (64, 64)), 0.0,
            ),
            axis=1, keepdims=True,
        )
        labels = lax.broadcasted_iota(jnp.int32, (64, 2 * ROW), 0)
        threshold = SHRINK_SCALE * jnp.sum(
            jnp.where(labels == tile_ref[...], column, 0.0), axis=0, keepdims=True
        )
        thr_s[0] = jnp.broadcast_to(threshold[:, :ROW], (8, ROW))
        thr_s[1] = jnp.broadcast_to(threshold[:, ROW:], (8, ROW))

    group_row = lax.broadcasted_iota(jnp.int32, (8, ROW), 0) // 2

    def block_rows(i):
        return pl.ds(pl.multiple_of(8 * i, 8), 8)

    def own_rows(out):
        kept = out[:, 0:ROW]
        for j in range(1, 4):
            kept = jnp.where(group_row == j, out[:, j * ROW : (j + 1) * ROW], kept)
        return kept

    def cells(h):
        return pl.ds(pl.multiple_of(ROW * h, ROW), ROW)

    def forward_start(field):
        for h in range(2):
            m_s[h] = dot(tf_ref[...], stacked(field[:, h * ROW : (h + 1) * ROW]))

        def step(i, carry):
            moved = jnp.concatenate([m_s[0, block_rows(i), :], m_s[1, block_rows(i), :]], axis=1)
            weights = kv[pl.ds(4 * i, 4)].reshape(512, 256)
            ab_s[block_rows(i), :] = own_rows(dot(moved.astype(BF16), weights, ((1,), (1,))))
            return carry

        for q in range(len(bounds) - 1):
            k_copy(0, q).wait()
            k_copy(1, q).wait()
            lo, hi = bounds[q] // 4, min(bounds[q + 1] // 4, 16)
            lax.fori_loop(lo, hi, step, 0, unroll=hi - lo)
        tail = jnp.concatenate([m_s[0, 128:136, :], m_s[1, 128:136, :]], axis=1).astype(BF16)
        ab_s[128:136, :] = dot(tail, kv[64], ((1,), (1,)))
        ab_s[136:144, :] = jnp.zeros((8, ROW), F32)

    def forward_half(field, h, adds):
        m_s[h] = dot(tf_ref[...], stacked(field))

        def step(i, carry):
            moved = m_s[h, block_rows(i), :].astype(BF16)
            weights = kv[pl.ds(4 * i, 4), :, cells(h)].reshape(512, ROW)
            kept = own_rows(dot(moved, weights, ((1,), (1,))))
            ab_s[block_rows(i), :] = ab_s[block_rows(i), :] + kept if adds else kept
            return carry

        lax.fori_loop(0, 16, step, 0, unroll=16)
        tail = dot(m_s[h, 128:136, :].astype(BF16), kv[64, :, cells(h)], ((1,), (1,)))
        ab_s[128:136, :] = ab_s[128:136, :] + tail if adds else tail

    def forward_end():
        out = dot3(ti_ref, ab_s[...])
        low = out[0:32] - pltpu.roll(out[64:96], 64, 1)
        high = pltpu.roll(out[32:64], 64, 1) - out[96:128]
        return jnp.where(left_half, low, high)

    def adjoint(packed, n):
        turned = pltpu.roll(packed, 64, 1)
        doubled = jnp.concatenate(
            [jnp.where(left_half, packed, turned), jnp.where(left_half, turned, packed)], axis=0
        )
        out = dot(ta_ref[...], stacked(doubled))
        l_s[...] = jnp.where(left_half, out[:ROWS], out[ROWS:])

        for h, order in ((1 - half, (4, 3, 5, 2, 6, 1, 7, 0)), (half, (4, 3, 5, 2, 6, 1, 7))):

            def step(i, carry):
                rows = l_s[block_rows(i), :]
                moved = jnp.concatenate(
                    [jnp.where(group_row == j, rows, 0.0) for j in range(4)], axis=1
                ).astype(BF16)
                weights = kv[pl.ds(4 * i, 4), :, cells(h)].reshape(512, ROW)
                q_s[h, block_rows(i), :] = dot(moved, weights)
                return carry

            lax.fori_loop(0, 16, step, 0, unroll=16)
            q_s[h, 128:136, :] = dot(l_s[128:136, :].astype(BF16), kv[64, :, cells(h)])
            q_s[h, 136:144, :] = jnp.zeros((8, ROW), F32)
            out = dot3(ts_ref, q_s[h])
            gp[n, pl.ds(8 * h, 8)] = out.reshape(8, 8, ROW)
            for j in order:
                p = 8 * h + (tb + j) % 8
                send(gp.at[n, p], rs_in.at[n, ms], {"sensor": p}, gr_ssem.at[n, 0], gr_rsem.at[n, 0])
        rs_in[n, ms] = gp[n, ms]

    def sum_start(n, packed):
        send1[n] = packed
        ya[n, my] = packed[0:16]
        zb[n, mz] = packed[16:32]
        for who in y_ids:
            send(send1.at[n, pl.ds(0, 16)], ya.at[n, my], who, ar_ssem.at[n, 0], ar_rsem.at[n, 0])
        for who in z_ids:
            send(send1.at[n, pl.ds(16, 16)], zb.at[n, mz], who, ar_ssem.at[n, 1], ar_rsem.at[n, 1])

    def sum_middle(n):
        wait_for(zb.at[n, pl.ds(0, NZ - 1)], ar_rsem.at[n, 1])
        part = jnp.sum(zb[n], axis=0)
        mid_b[n] = part
        yb[n, my] = part
        for who in y_ids:
            send(mid_b.at[n], yb.at[n, my], who, ar_ssem.at[n, 2], ar_rsem.at[n, 2])
        wait_for(ya.at[n, pl.ds(0, NY - 1)], ar_rsem.at[n, 0])
        part = jnp.sum(ya[n], axis=0)
        mid_a[n] = part
        za[n, mz] = part
        for who in z_ids:
            send(mid_a.at[n], za.at[n, mz], who, ar_ssem.at[n, 3], ar_rsem.at[n, 3])

    def sum_end(n):
        wait_for(za.at[n, pl.ds(0, NZ - 1)], ar_rsem.at[n, 3])
        wait_for(yb.at[n, pl.ds(0, NY - 1)], ar_rsem.at[n, 2])
        return jnp.concatenate([jnp.sum(za[n], axis=0), jnp.sum(yb[n], axis=0)], axis=0)

    def scalars_start(n, one, two):
        sc_send[n, pl.ds(0, 1), :] = one
        sc_send[n, pl.ds(1, 1), :] = two
        sy[n, my, pl.ds(0, 1), :] = one
        sy[n, my, pl.ds(1, 1), :] = two
        for who in y_ids:
            send(sc_send.at[n], sy.at[n, my], who, sc_ssem.at[n, 0], sc_rsem.at[n, 0])

    def scalars_middle(n):
        wait_for(sy.at[n, pl.ds(0, NY - 1)], sc_rsem.at[n, 0])
        part = jnp.sum(sy[n], axis=0)
        sc_mid[n] = part
        sz[n, mz] = part
        for who in z_ids:
            send(sc_mid.at[n], sz.at[n, mz], who, sc_ssem.at[n, 1], sc_rsem.at[n, 1])

    def response_start(n, packed):
        row = jnp.sum(packed * packed, axis=0, keepdims=True)
        rs_send[n] = row
        rs_buf[n, ms] = row
        for p in s_nums:
            send(rs_send.at[n], rs_buf.at[n, ms], {"sensor": p}, rs_ssem.at[n], rs_rsem.at[n])

    def step_size(n):
        wait_for(sz.at[n, pl.ds(0, NZ - 1)], sc_rsem.at[n, 1])
        wait_for(rs_buf.at[n, pl.ds(0, NSEN - 1)], rs_rsem.at[n])
        sums = jnp.sum(sz[n], axis=0)
        total = jnp.sum(sums, axis=1, keepdims=True)
        response = jnp.sum(jnp.sum(rs_buf[n], axis=0), axis=1, keepdims=True)
        return total[0:1] / (response + total[1:2] + TINY)

    def scatter_end(n):
        wait_for(rs_in.at[n, pl.ds(0, NSEN - 1)], gr_rsem.at[n, 0])
        return jnp.sum(rs_in[n], axis=0)

    def gather_forward(n, piece):
        b_s[1 + n] = piece
        g_s[n, ms] = piece
        src, dst = b_s.at[1 + n], g_s.at[n, ms]
        for j in (4, 3, 5, 2, 6, 1, 7, 0):
            who = {"sensor": 8 * (1 - half) + (tb + j) % 8}
            send(src, dst, who, gr_ssem.at[n, 1], gr_rsem.at[n, 1])
        for j in (4, 3, 5, 2, 6, 1, 7):
            who = {"sensor": 8 * half + (tb + j) % 8}
            send(src, dst, who, gr_ssem.at[n, 2], gr_rsem.at[n, 2])
        wait_for(g_s.at[n, pl.ds(0, 7)], gr_rsem.at[n, 2])
        forward_half(g_s[n, pl.ds(8 * half, 8)].reshape(NT, ROW), half, False)
        wait_for(g_s.at[n, pl.ds(0, 8)], gr_rsem.at[n, 1])
        send(g_s.at[n, pl.ds(8, 8)], gh_n.at[n], nxt_id, gh_ssem.at[n, 0], gh_rsem.at[n, 0])
        send(g_s.at[n, pl.ds(0, 8)], gh_s.at[n], prv_id, gh_ssem.at[n, 1], gh_rsem.at[n, 1])
        forward_half(g_s[n, pl.ds(8 * (1 - half), 8)].reshape(NT, ROW), 1 - half, True)
        return forward_end()

    def halo(n):
        wait_for(gh_n.at[n], gh_rsem.at[n, 0])
        wait_for(gh_s.at[n], gh_rsem.at[n, 1])
        return gh_n[n].reshape(NT, ROW), gh_s[n].reshape(NT, ROW)

    def jumps(dst, above, first, second, below):
        rows = (first, second)
        for r in range(2):
            dst[r] = jnp.where(linked[0][r], pltpu.roll(rows[r], ROW - 1, 1) - rows[r], 0.0)
            dst[2 + r] = jnp.where(linked[1][r], pltpu.roll(rows[r], 1, 1) - rows[r], 0.0)
            north = above if r == 0 else first
            south = second if r == 0 else below
            dst[4 + r] = jnp.where(linked[2][r], north - rows[r], 0.0)
            dst[6 + r] = jnp.where(linked[3][r], south - rows[r], 0.0)

    def squares(refs):
        total = jnp.zeros((1, ROW), F32)
        for value in refs:
            total = total + jnp.sum(value * value, axis=0, keepdims=True)
        return total

    def divergence(v):
        for r in range(2):
            total = jnp.where(linked[1][r], pltpu.roll(v[r], 1, 1), 0.0)
            total = total + jnp.where(linked[0][r], pltpu.roll(v[2 + r], ROW - 1, 1), 0.0)
            if r == 0:
                total = total + jnp.where(linked[3][0], v[5], 0.0)
            else:
                total = total + jnp.where(linked[2][1], v[6], 0.0)
            for k in range(4):
                total = total - jnp.where(linked[k][r], v[2 * k + r], 0.0)
            dt_s[8 * r : 8 * r + 8] = total.reshape(8, 8, ROW)

    load(0).wait()
    load(1).wait()
    forward_start(x0_ref[...])
    load(2).wait()
    first_sum = forward_end()
    pl.semaphore_wait(barrier, len(everyone))
    sum_start(0, first_sum)
    prepare()
    own = cell * (2 * ROW) + lax.broadcasted_iota(jnp.int32, (1, 2 * ROW), 1)
    linked = [[None, None] for _ in range(4)]
    edges = []
    for k in range(4):
        both = jnp.where(nb_ref[pl.ds(k, 1), :] != own, 1.0, 0.0)
        linked[k][0] = both[:, :ROW] > 0.5
        linked[k][1] = both[:, ROW:] > 0.5
        if k >= 2:
            edges.append(both[:, :ROW] if k == 2 else both[:, ROW:])
    edge_link = jnp.where(half == 0, edges[0], edges[1]) > 0.5
    load(6).wait()
    sum_middle(0)
    lanes = pl.multiple_of(ROW * (1 - half), ROW)
    times = pl.multiple_of(8 * tb, 8)
    send(
        m0_ref.at[3 - half, pl.ds(times, 8), pl.ds(lanes, ROW)], h_m, edge_id,
        h_ssem.at[0], h_rsem.at[0],
    )
    send(thr_s.at[1 - half], h_t, edge_id, h_ssem.at[1], h_rsem.at[1])
    divergence([m0_ref[k, :, r * ROW : (r + 1) * ROW] for k in range(4) for r in range(2)])
    for i in (7, 8, 9):
        load(i).wait()
    observed = jnp.concatenate([obs_ref[0:32], obs_ref[32:64]], axis=1)
    misfit = sum_end(0) - observed

    adjoint(misfit, 0)
    send(x0_ref.at[:, pl.ds(ROW, ROW)], hx_n, nxt_id, h_ssem.at[2], h_rsem.at[2])
    send(x0_ref.at[:, pl.ds(0, ROW)], hx_s, prv_id, h_ssem.at[3], h_rsem.at[3])
    wait_for(h_m, h_rsem.at[0])
    wait_for(h_t, h_rsem.at[1])
    extra = dt_s[ms] + jnp.where(edge_link, h_m[...], 0.0)
    piece = scatter_end(0)
    b_s[0] = piece
    sum_start(1, gather_forward(0, piece + extra))
    above, below = halo(0)
    grad_a = g_s[0, 0:8].reshape(NT, ROW)
    grad_b = g_s[0, 8:16].reshape(NT, ROW)
    jumps(gj_s, above, grad_a, grad_b, below)
    scalars_start(0, squares([grad_a, grad_b]), squares([gj_s[i] for i in range(8)]))
    sum_middle(1)
    scalars_middle(0)
    response = sum_end(1)
    response_start(0, response)
    adjoint(response, 1)
    wait_for(hx_n, h_rsem.at[2])
    wait_for(hx_s, h_rsem.at[3])
    jumps(jump_s, hx_n[...], x0_ref[:, 0:ROW], x0_ref[:, ROW:], hx_s[...])
    size = step_size(0)
    penalty = []
    thresholds = [thr_s[0, 0:1], thr_s[1, 0:1]]
    for i in range(8):
        moved = jump_s[i] - size * gj_s[i]
        jump_s[i] = moved
        limit = thresholds[i % 2]
        shifted = moved + m0_ref[i // 2, :, (i % 2) * ROW : (i % 2 + 1) * ROW]
        shrunk = jnp.maximum(shifted - limit, 0.0) - jnp.maximum(-shifted - limit, 0.0)
        rest = shifted - shrunk
        mult_s[i] = rest
        penalty.append(moved - shrunk + rest)
    divergence(penalty)
    moved = -jump_s[4 + 3 * half, pl.ds(times, 8), :]
    shifted = moved + h_m[...]
    limit = h_t[...]
    shrunk = jnp.maximum(shifted - limit, 0.0) - jnp.maximum(-shifted - limit, 0.0)
    extra = dt_s[ms] + jnp.where(edge_link, moved - shrunk + (shifted - shrunk), 0.0)
    est_ref[:, 0:ROW] = x0_ref[:, 0:ROW] - size * g_s[0, 0:8].reshape(NT, ROW)
    est_ref[:, ROW:] = x0_ref[:, ROW:] - size * g_s[0, 8:16].reshape(NT, ROW)

    piece = b_s[0] - size * scatter_end(1)
    sum_start(2, gather_forward(1, piece + extra))
    above, below = halo(1)
    grad_a = g_s[1, 0:8].reshape(NT, ROW)
    grad_b = g_s[1, 8:16].reshape(NT, ROW)
    jumps(gj_s, above, grad_a, grad_b, below)
    scalars_start(1, squares([grad_a, grad_b]), squares([gj_s[i] for i in range(8)]))
    sum_middle(2)
    scalars_middle(1)
    response_start(1, sum_end(2))
    size = step_size(1)
    est_ref[:, 0:ROW] = est_ref[:, 0:ROW] - size * g_s[1, 0:8].reshape(NT, ROW)
    est_ref[:, ROW:] = est_ref[:, ROW:] - size * g_s[1, 8:16].reshape(NT, ROW)
    for i in range(8):
        shifted = jump_s[i] - size * gj_s[i] + mult_s[i]
        limit = thresholds[i % 2]
        shrunk = jnp.maximum(shifted - limit, 0.0) - jnp.maximum(-shifted - limit, 0.0)
        k, r = i // 2, i % 2
        aux_ref[k, :, r * ROW : (r + 1) * ROW] = shrunk
        mul_ref[k, :, r * ROW : (r + 1) * ROW] = shifted - shrunk

    for i, view in enumerate((h_m, h_t, hx_n, hx_s)):
        wait_for(view, h_ssem.at[i])
    for n in range(3):
        wait_for(ya.at[n, pl.ds(0, NY - 1)], ar_ssem.at[n, 0])
        wait_for(zb.at[n, pl.ds(0, NZ - 1)], ar_ssem.at[n, 1])
        wait_for(yb.at[n, pl.ds(0, NY - 1)], ar_ssem.at[n, 2])
        wait_for(za.at[n, pl.ds(0, NZ - 1)], ar_ssem.at[n, 3])
    for n in range(2):
        wait_for(sy.at[n, pl.ds(0, NY - 1)], sc_ssem.at[n, 0])
        wait_for(sz.at[n, pl.ds(0, NZ - 1)], sc_ssem.at[n, 1])
        wait_for(rs_buf.at[n, pl.ds(0, NSEN - 1)], rs_ssem.at[n])
        wait_for(rs_in.at[n, pl.ds(0, NSEN - 1)], gr_ssem.at[n, 0])
        wait_for(g_s.at[n, pl.ds(0, 8)], gr_ssem.at[n, 1])
        wait_for(g_s.at[n, pl.ds(0, 7)], gr_ssem.at[n, 2])
        wait_for(gh_n.at[n], gh_ssem.at[n, 0])
        wait_for(gh_s.at[n], gh_ssem.at[n, 1])


def finish(est, aux, mul, est_out, aux_out, mul_out, sems):
    copies = [
        pltpu.make_async_copy(src, dst, sems.at[i])
        for i, (src, dst) in enumerate(((aux, aux_out), (mul, mul_out), (est, est_out)))
    ]
    for copy in copies:
        copy.start()
    for copy in copies:
        copy.wait()


def per_device(kernel, observed, start_model, start_multiplier, neighbours, tile, weight):
    hbm = pl.BlockSpec(memory_space=pltpu.HBM)
    vmem = pl.BlockSpec(memory_space=pltpu.VMEM)
    scratch = lambda *shape, dtype=F32: pltpu.VMEM(shape, dtype)
    dma = lambda *shape: pltpu.SemaphoreType.DMA(shape)
    analysis, back, synthesis, closing = (jnp.asarray(t) for t in tables())
    inputs = (
        kernel, observed, start_model, start_multiplier, neighbours, tile.reshape(1, 256),
        weight.reshape(1, 64), analysis, back, synthesis, closing,
    )
    results = pl.pallas_call(
        body,
        out_shape=(
            jax.ShapeDtypeStruct((NT, 256), F32),
            jax.ShapeDtypeStruct((4, NT, 256), F32),
            jax.ShapeDtypeStruct((4, NT, 256), F32),
        ),
        in_specs=[hbm] * 11,
        out_specs=(vmem, vmem, vmem),
        scratch_shapes=[
            scratch(NF, 128, 256, dtype=BF16),
            scratch(NT, 64),
            scratch(NT, 256),
            scratch(4, NT, 256),
            scratch(4, 256, dtype=jnp.int32),
            scratch(1, 256, dtype=jnp.int32),
            scratch(1, 64),
            scratch(ROWS, 256, dtype=BF16),
            scratch(2 * ROWS, 256, dtype=BF16),
            scratch(2, 128, ROWS, dtype=BF16),
            scratch(2, NT, ROWS, dtype=BF16),
            scratch(2, ROWS, ROW),
            scratch(ROWS, ROW),
            scratch(ROWS, ROW),
            scratch(2, ROWS, ROW),
            scratch(3, 32, ROW),
            scratch(3, NY, 16, ROW),
            scratch(3, NZ, 16, ROW),
            scratch(3, NZ, 16, ROW),
            scratch(3, NY, 16, ROW),
            scratch(3, 16, ROW),
            scratch(3, 16, ROW),
            scratch(2, 2, ROW),
            scratch(2, 2, ROW),
            scratch(2, NY, 2, ROW),
            scratch(2, NZ, 2, ROW),
            scratch(2, 1, ROW),
            scratch(2, NSEN, 1, ROW),
            scratch(2, 16, 8, ROW),
            scratch(2, NSEN, 8, ROW),
            scratch(2, 16, 8, ROW),
            scratch(3, 8, ROW),
            scratch(16, 8, ROW),
            scratch(2, 8, ROW),
            scratch(8, ROW),
            scratch(8, ROW),
            scratch(NT, ROW),
            scratch(NT, ROW),
            scratch(2, 8, 8, ROW),
            scratch(2, 8, 8, ROW),
            scratch(8, NT, ROW),
            scratch(8, NT, ROW),
            scratch(8, NT, ROW),
            dma(2, 5),
            dma(10),
            dma(4),
            dma(4),
            dma(3, 4),
            dma(3, 4),
            dma(2, 2),
            dma(2, 2),
            dma(2),
            dma(2),
            dma(2, 3),
            dma(2, 3),
            dma(2, 2),
            dma(2, 2),
        ],
        compiler_params=pltpu.CompilerParams(
            collective_id=0, has_side_effects=True, vmem_limit_bytes=MAIN_VMEM
        ),
        name="inversion",
    )(*(pltpu.with_memory_space_constraint(x, pltpu.HBM) for x in inputs))
    return pl.pallas_call(
        finish,
        out_shape=tuple(jax.ShapeDtypeStruct(r.shape, F32) for r in results),
        in_specs=[vmem] * 3,
        out_specs=(hbm, hbm, hbm),
        scratch_shapes=[dma(3)],
        compiler_params=pltpu.CompilerParams(vmem_limit_bytes=1024 * 1024),
        name="finish",
    )(*results)


def solution(mesh):
    split_mesh = Mesh(mesh.devices.reshape(NY, NZ, NSEN), ("y", "zh", "sensor"))
    cells = ("y", "zh")
    in_specs = (
        P(None, None, "sensor", cells),
        P(None, "sensor"),
        P(None, cells),
        P(None, None, cells),
        P(None, cells),
        P(cells),
        P(),
    )
    out_specs = (P(None, cells), P(None, None, cells), P(None, None, cells))
    return jax.shard_map(
        per_device, mesh=split_mesh, in_specs=in_specs, out_specs=out_specs, check_vma=False
    )
```
